512 devices in a mesh: tm: 64 (over y, z), pad: 8 (over x, core).
Axes of the slice: x: 4, y: 4, z: 16, core: 2. Of those that a mesh axis runs over, the one named last changes fastest.
Arguments:
- charge: float32 [8, 32768], P('pad', 'tm'), may hold values from 0.3 to 3
- pad_row: int32 [8, 32768], P('pad', 'tm'), may hold values from 0 to 9
- pad_column: int32 [8, 32768], P('pad', 'tm'), may hold values from 0 to 65
- time_bin: int32 [8, 32768], P('pad', 'tm'), may hold values from 0 to 1023
- slab_owner: int32 [8, 32768, 1], P('pad', 'tm'), may hold values from 0 to 63; in each aligned block of 512 rows (0 to 511, 512 to 1023, ..., all dimensions but the last counted through in order) at most 16 rows name the same one
- block_count: int32 [8, 256], P('pad', 'tm'), may hold values from 1 to 128
- shaping: float32 [1024], replicated, may hold values from 0.02 to 1
- response: float32 [3, 3], replicated, may hold values from 0.05 to 1
Outputs:
- signal: float32 [80, 66, 65536], P('pad', None, 'tm')
The draws below stay inside these ranges and needn't reach their ends.
Inputs may be any that keep to these rules, and one draw needn't show every extreme that they name: `slab_owner`: among the cluster rows of one device, at most 16 name the same time slab, a bound that some of them reach. Only the first block_count rows of each block of 128 cluster rows hold clusters.
All inputs are finite; a program needn't handle non-finite values.
Results may differ from the reference program's by a relative error of at most 0.0003.
Values sent between devices are 32-bit elements; how exact they have to be, the bound alone decides.
A program may use at most 64 MiB of HBM per device.

```python
import math
import jax
import jax.numpy as jnp
import numpy as np
from jax import lax

PROWS = 80
PPR = 66
T_DEV = 1024
KLEN = 1024
SRC_ROWS = 512
CAP = 16
SRC_ALL = 32768
BLK_ALL = 256
RG = 10
N_TM = 64
N_PAD = 8


def with_ends(entries, rng, smallest, high):
    dims = entries.shape
    index_at = [jax.random.randint(jax.random.fold_in(rng, axis), (), 0, dims[axis]) for axis in range(len(dims))]
    entries = entries.at[tuple(index_at)].set(smallest)
    longest = dims.index(max(dims))
    index_at[longest] = (index_at[longest] + 1) % dims[longest]
    return entries.at[tuple(index_at)].set(high)


def levels(stream_key, extent, cuts, least, top_value):
    def one(dim, shards_of):
        steps = jax.random.uniform(jax.random.fold_in(jax.random.fold_in(stream_key, 6), dim), (shards_of,), jnp.float32, least / len(cuts), top_value / len(cuts))
        return jnp.repeat(jnp.exp(steps), extent[dim] // shards_of).reshape((-1,) + (1,) * (len(extent) - dim - 1))

    factor_of = one(*cuts[0])
    for cut in cuts[1:]:
        factor_of = factor_of * one(*cut)
    return factor_of


def assign_block(stream_key, own, number, rows, number_of, top, most, skew):
    sequence = jax.random.permutation(stream_key, number_of)
    packed, usual = load_shares(number_of, rows * top, most, skew, True), load_shares(number_of, rows * top, most, skew, False)
    places = jnp.arange(number_of)

    def named(tallies, offset_by):
        used = int((tallies > 0).sum())
        fixed = max(1, used // 4)
        passed = fixed + (places - fixed + offset_by * (used - fixed)) % max(1, number_of - fixed)
        return jnp.zeros((number_of,), jnp.int32).at[sequence[jnp.where(places < fixed, places, passed)]].set(jnp.asarray(tallies, jnp.int32))

    tallies = jnp.where(number % 4 == 0, named(packed, number // 4), named(usual, number - number // 4 - 1))
    mixed = jax.random.permutation(jax.random.fold_in(own, 3), number_of)
    source_of, sink = mixed[0:number_of // 2 * 2:2], mixed[1:number_of // 2 * 2:2]
    slack = jnp.minimum(tallies[source_of] - 1, most - tallies[sink]) // 2
    slack = jnp.where((source_of == sequence[0]) | (sink == sequence[0]) | (tallies[sink] == 0), 0, jnp.maximum(slack, 0))
    passed = jax.random.randint(jax.random.fold_in(own, 4), (number_of // 2,), 0, 1 << 20) % (slack + 1)
    tallies = tallies.at[source_of].add(-passed).at[sink].add(passed)
    labels = jnp.searchsorted(jnp.cumsum(tallies), jnp.arange(rows * top), side="right").astype(jnp.int32)
    table = labels.reshape(top, rows).T
    table = table[jax.random.permutation(jax.random.fold_in(own, 1), rows)]
    offset_by = jax.random.randint(jax.random.fold_in(own, 2), (rows, 1), 0, top)
    return jnp.take_along_axis(table, (jnp.arange(top)[None, :] + offset_by) % top, axis=1)


def load_shares(count, total, reach, slope, full):
    portions = [(1 << 20) // math.isqrt(grade ** slope) + 1 for grade in range(1, count + 1)]
    largest = reach if full else min(reach, max(-(-total // count), total * portions[0] // sum(portions)))
    least = 1 if total - largest >= count - 1 else 0
    holding, spare = [largest] + [least] * (count - 1), total - largest - least * (count - 1)
    while spare > 0:
        candidates = [i for i in range(1, count) if holding[i] < largest] or [i for i in range(1, count) if holding[i] < reach]
        whole, left = sum([portions[i] for i in candidates]), spare
        for i in candidates:
            extra = min(reach - holding[i], max(1, left * portions[i] // whole), spare)
            holding[i] = holding[i] + extra
            spare = spare - extra
    return np.array(holding)


def setup_inputs(seed: int = 0) -> dict:
    streams_of = jax.random.split(jax.random.key(seed), 9)
    charge = jnp.clip(jnp.exp(math.log(3.0) - 2.3025851 * jax.random.uniform(streams_of[0], (N_PAD, SRC_ALL), jnp.float32) ** levels(streams_of[0], (N_PAD, SRC_ALL), ((0, 8), (1, 64)), -0.2, 0.2)), 0.3, 3.0)
    pad_row = with_ends(jax.random.randint(streams_of[1], (N_PAD, SRC_ALL), 0, RG), jax.random.fold_in(streams_of[1], 1), 0, RG - 1).astype(jnp.int32)
    pad_column = with_ends(jax.random.randint(streams_of[2], (N_PAD, SRC_ALL), 0, PPR), jax.random.fold_in(streams_of[2], 1), 0, PPR - 1).astype(jnp.int32)
    time_bin = with_ends(jax.random.randint(streams_of[3], (N_PAD, SRC_ALL), 0, T_DEV), jax.random.fold_in(streams_of[3], 1), 0, T_DEV - 1).astype(jnp.int32)
    slab_owner_keys = jax.random.split(jax.random.fold_in(streams_of[4], 1), N_PAD * SRC_ALL // SRC_ROWS)
    slab_owner_turns = jax.random.permutation(jax.random.fold_in(streams_of[4], 3), N_PAD * SRC_ALL // SRC_ROWS)
    slab_owner = jax.vmap(lambda own, number: assign_block(jax.random.fold_in(streams_of[4], 2), own, number, SRC_ROWS, N_TM, 1, CAP, 2))(slab_owner_keys, slab_owner_turns).reshape((N_PAD, SRC_ALL, 1))
    block_count = with_ends(jax.random.randint(streams_of[5], (N_PAD, BLK_ALL), 1, 129), jax.random.fold_in(streams_of[5], 1), 1, 128).astype(jnp.int32)
    shaping = jnp.clip(jax.random.uniform(streams_of[6], (KLEN,), jnp.float32, 0.02, 1.0), 0.02, 1.0)
    response = jnp.clip(jax.random.uniform(streams_of[7], (3, 3), jnp.float32, 0.05, 1.0), 0.05, 1.0)
    return dict(charge=charge, pad_row=pad_row, pad_column=pad_column, time_bin=time_bin, slab_owner=slab_owner, block_count=block_count, shaping=shaping, response=response)


def lag_tables(shaping):
    width = 128
    count = shaping.shape[0] // width + 1
    longer = jnp.concatenate([jnp.zeros((width,), shaping.dtype), shaping, jnp.zeros((2 * width,), shaping.dtype)])
    tables = []
    for lag_block in range(count):
        base = width + width * lag_block
        line = jnp.concatenate([longer[base:base + width], jnp.zeros((1,), shaping.dtype), longer[base - width + 1:base]])
        tiled = jnp.tile(line, width)[: width * (2 * width - 1)].reshape(width, 2 * width - 1)
        tables.append(tiled[:, :width])
    return tables


def shape_time(current, previous, tables):
    cells, bins = current.shape
    blocks = bins // 128
    extended = jnp.concatenate([previous.reshape(cells, blocks, 128), current.reshape(cells, blocks, 128)], axis=1)
    result = jnp.zeros((cells * blocks, 128), current.dtype)
    for lag_block, table in enumerate(tables):
        piece = extended[:, blocks - lag_block:2 * blocks - lag_block].reshape(cells * blocks, 128)
        result = result + jnp.dot(piece, table, precision=lax.Precision.HIGHEST, preferred_element_type=current.dtype)
    return result.reshape(cells, bins)


def spread(padded, response):
    row_count = padded.shape[0] - 2
    columns = padded.shape[1]
    wide = jnp.pad(padded, ((0, 0), (1, 1), (0, 0)))
    result = jnp.zeros((row_count, columns, padded.shape[2]), padded.dtype)
    for above in range(3):
        for beside in range(3):
            result = result + response[above, beside] * wide[above:above + row_count, beside:beside + columns]
    return result


def reference(charge, pad_row, pad_column, time_bin, slab_owner, block_count, shaping, response):
    cells = (PROWS // N_PAD) * PPR
    bins = T_DEV * N_TM
    tables = lag_tables(shaping)

    def one_group(group):
        charge_g, row_g, column_g, bin_g, owner_g, count_g = group
        total = charge_g.shape[0]
        live = (lax.broadcasted_iota(jnp.int32, (total // 128, 128), 1) < count_g[:, None]).reshape(total)
        cell = (row_g * PPR + column_g).astype(jnp.int32)
        moment = (owner_g * T_DEV + bin_g).astype(jnp.int32)
        grid = jnp.zeros((cells, bins), charge_g.dtype).at[cell, moment].add(jnp.where(live, charge_g, 0.0))
        return shape_time(grid, jnp.zeros_like(grid), tables)

    shaped = lax.map(one_group, (charge, pad_row, pad_column, time_bin, slab_owner[:, :, 0], block_count))
    shaped = shaped.reshape(PROWS, PPR, bins)
    padded = jnp.pad(shaped, ((1, 1), (0, 0), (0, 0)))
    return spread(padded, response)
```

```python
import functools

import jax
import jax.numpy as jnp
from jax import lax
from jax.experimental import pallas as pl
from jax.experimental.pallas import tpu as pltpu
from jax.sharding import PartitionSpec as P

PROWS = 80
PPR = 66
STRIDE = 72
CAP = 16
FIELDS = 4
HALF = FIELDS * CAP
F32 = jnp.float32
BF16 = jnp.bfloat16
LANES = 128
TILE = 256
NT = (((1,), (1,)), ((), ()))


def split(x):
    high = x.astype(BF16)
    return high, (x - high.astype(F32)).astype(BF16)


def route_kernel(last_row, charge_ref, row_ref, column_ref, bin_ref, owner_ref, count_ref, out_ref):
    slabs = out_ref.shape[0]
    clusters = charge_ref.shape[1]
    lane = lax.broadcasted_iota(jnp.int32, (1, clusters), 1)
    limit = jnp.zeros((1, clusters), jnp.int32)
    for block in range(clusters // LANES):
        limit = jnp.where(lane // LANES == block, count_ref[0, block], limit)
    live = lane % LANES < limit
    row = row_ref[...]
    owner = jnp.where(live, owner_ref[...], slabs)
    mine = owner == lax.broadcasted_iota(jnp.int32, (slabs, clusters), 0)
    upper = row == last_row
    lower = row == 0
    middle = jnp.logical_not(jnp.logical_or(upper, lower))
    kinds = [jnp.where(jnp.logical_and(mine, kind), 1.0, 0.0) for kind in (upper, middle, lower)]
    stacked = jnp.concatenate(kinds, axis=0).astype(BF16)
    earlier = (
        lax.broadcasted_iota(jnp.int32, (clusters, clusters), 0)
        < lax.broadcasted_iota(jnp.int32, (clusters, clusters), 1)
    ).astype(F32).astype(BF16)
    ranks = jnp.dot(stacked, earlier, preferred_element_type=F32)
    uppers = jnp.sum(kinds[0], axis=1, keepdims=True)
    places = (
        kinds[0] * ranks[:slabs]
        + kinds[1] * (uppers + ranks[slabs : 2 * slabs])
        + kinds[2] * ((CAP - 1) - ranks[2 * slabs :])
    )
    place = jnp.sum(places, axis=0, keepdims=True).astype(jnp.int32)
    slot = lax.broadcasted_iota(jnp.int32, (CAP, clusters), 0)
    here = place == slot
    fields = (charge_ref[...], row.astype(F32), column_ref[...].astype(F32), bin_ref[...].astype(F32))
    spread_out = jnp.concatenate([jnp.where(here, field, 0.0) for field in fields], axis=0)
    own = lax.dot_general(
        jnp.where(mine, 1.0, 0.0), spread_out, NT, precision=lax.Precision.HIGHEST, preferred_element_type=F32
    )
    slab = lax.broadcasted_iota(jnp.int32, own.shape, 0)
    before = jnp.where(slab == 0, 0.0, pltpu.roll(own, 1, 0))
    out_ref[...] = jnp.concatenate([own, before], axis=1)


def route(charge, row, column, time, owner, count, slabs, last_row):
    return pl.pallas_call(
        functools.partial(route_kernel, last_row),
        out_shape=jax.ShapeDtypeStruct((slabs, 2 * HALF), F32),
        in_specs=[pl.BlockSpec(memory_space=pltpu.VMEM)] * 5 + [pl.BlockSpec(memory_space=pltpu.SMEM)],
        out_specs=pl.BlockSpec(memory_space=pltpu.VMEM),
        name="route",
    )(charge, row, column, time, owner, count)


def zigzag(step, size):
    half = (step + 1) // 2
    away = jnp.where(step % 2 == 0, half, -half)
    return lax.rem(size // 2 + away + size, size)


def exchange_kernel(rows_y, rows_z, send_ref, out_ref, send_sem, recv_sem, side_send, side_recv):
    slabs = send_ref.shape[0]
    groups = lax.axis_size("pad")
    me = lax.axis_index("tm")
    group = lax.axis_index("pad")
    above = lax.rem(group + 1, groups)
    below = lax.rem(group + groups - 1, groups)
    my_y, my_z = me // rows_z, lax.rem(me, rows_z)

    def peer_of(step):
        z = lax.rem(my_z + zigzag(step // rows_y, rows_z), rows_z)
        y = lax.rem(my_y + zigzag(lax.rem(step, rows_y), rows_y), rows_y)
        return y * rows_z + z

    barrier = pltpu.get_barrier_semaphore()

    def greet(step, carry):
        pl.semaphore_signal(
            barrier, inc=1, device_id=(peer_of(step), group), device_id_type=pl.DeviceIdType.MESH
        )
        return carry

    lax.fori_loop(0, slabs - 1, greet, 0)
    for side in (above, below):
        pl.semaphore_signal(barrier, inc=1, device_id=(me, side), device_id_type=pl.DeviceIdType.MESH)
    out_ref[1, pl.ds(me, 1)] = send_ref[pl.ds(me, 1)]
    pl.semaphore_wait(barrier, slabs + 1)

    def send(step, carry):
        peer = peer_of(step)
        pltpu.make_async_remote_copy(
            src_ref=send_ref.at[pl.ds(peer, 1)],
            dst_ref=out_ref.at[1, pl.ds(me, 1)],
            send_sem=send_sem,
            recv_sem=recv_sem,
            device_id=(peer, group),
            device_id_type=pl.DeviceIdType.MESH,
        ).start()
        return carry

    lax.fori_loop(0, slabs - 1, send, 0)
    whole = pltpu.make_async_copy(
        send_ref.at[pl.ds(0, slabs - 1)], out_ref.at[1, pl.ds(0, slabs - 1)], recv_sem
    )
    whole.wait()
    copies = []
    for index, (side, place) in enumerate(((above, 0), (below, 2))):
        copies.append(
            pltpu.make_async_remote_copy(
                src_ref=out_ref.at[1],
                dst_ref=out_ref.at[place],
                send_sem=side_send.at[index],
                recv_sem=side_recv.at[index],
                device_id=(me, side),
                device_id_type=pl.DeviceIdType.MESH,
            )
        )
        copies[-1].start()
    pltpu.make_async_copy(
        send_ref.at[pl.ds(0, slabs - 1)], out_ref.at[1, pl.ds(0, slabs - 1)], send_sem
    ).wait()
    for copy in copies:
        copy.wait()

    @pl.when(group == 0)
    def _():
        out_ref[0] = jnp.zeros(out_ref.shape[1:], F32)

    @pl.when(group == groups - 1)
    def _():
        out_ref[2] = jnp.zeros(out_ref.shape[1:], F32)


def exchange(rows, rows_y):
    slabs, width = rows.shape
    return pl.pallas_call(
        functools.partial(exchange_kernel, rows_y, slabs // rows_y),
        out_shape=jax.ShapeDtypeStruct((3, slabs, width), F32),
        in_specs=[pl.BlockSpec(memory_space=pltpu.VMEM)],
        out_specs=pl.BlockSpec(memory_space=pltpu.VMEM),
        scratch_shapes=[
            pltpu.SemaphoreType.DMA,
            pltpu.SemaphoreType.DMA,
            pltpu.SemaphoreType.DMA((2,)),
            pltpu.SemaphoreType.DMA((2,)),
        ],
        compiler_params=pltpu.CompilerParams(collective_id=0, has_side_effects=True),
        name="exchange",
    )(rows)


def digitize_kernel(
    row_count, bins, recv_ref, shaping_ref, response_ref, out_ref,
    high, low, table_high, table_low, wide, hits, parts, shaped, edges, held, columns,
):
    slabs = recv_ref.shape[1]
    step = pl.program_id(0)
    cells = row_count * STRIDE
    slots = slabs * CAP
    pairs = CAP // 2
    chunk = 4 * slabs

    def sides(which):
        flipped = jnp.transpose(recv_ref[which])
        return [
            [
                jnp.concatenate(
                    [
                        flipped[HALF * slab + CAP * field : HALF * slab + CAP * field + pairs],
                        flipped[HALF * slab + CAP * field + pairs : HALF * slab + CAP * (field + 1)],
                    ],
                    axis=1,
                )
                for field in range(FIELDS)
            ]
            for slab in range(2)
        ]

    def hit_rows(which, slab, slot):
        at = HALF * slab + CAP * 3 + (slot % 2) * pairs + slot // 2
        column = recv_ref[which, :, at : at + 1].astype(jnp.int32)
        moment = lax.broadcasted_iota(jnp.int32, (slabs, bins), 1)
        return jnp.where(moment == column, 1.0, 0.0).astype(BF16)

    @pl.when(step == 0)
    def _():
        lags = shaping_ref.shape[1]
        line = jnp.concatenate(
            [jnp.zeros((1, TILE), F32), shaping_ref[...], jnp.zeros((1, TILE), F32)], axis=1
        )
        rolled = pltpu.roll(
            jnp.broadcast_to(line, (TILE, lags + 2 * TILE)), 0, 1, stride=1, stride_axis=0
        )
        top, rest = split(rolled)
        for block in range(lags // TILE + 1):
            at = lags + TILE - TILE * block
            table_high[TILE * block : TILE * (block + 1)] = top[:, at : at + TILE]
            table_low[TILE * block : TILE * (block + 1)] = rest[:, at : at + TILE]

        own = sides(1)
        pad = lax.broadcasted_iota(jnp.int32, (STRIDE, 2 * slabs), 0)
        for slab in range(2):
            charge, row, column, _ = own[slab]
            for pair in range(pairs):
                there = pad == column[pair : pair + 1].astype(jnp.int32)
                lanes = slice(2 * slabs * pair, 2 * slabs * (pair + 1))
                for lead in range(0, row_count, 2):
                    both = []
                    for r in (lead, lead + 1):
                        value = jnp.where(row[pair : pair + 1] == float(r), charge[pair : pair + 1], 0.0)
                        both.append(jnp.where(there, value, 0.0))
                    top, rest = split(jnp.concatenate(both, axis=0))
                    at = lead * STRIDE
                    wide[at : at + 2 * STRIDE, lanes] = top
                    wide[cells + at : cells + at + 2 * STRIDE, lanes] = rest
            for slot in range(CAP):
                hits[slabs * slot : slabs * (slot + 1)] = hit_rows(1, slab, slot)
            base = bins * (1 - slab)

            def lay(block, carry):
                at = pl.multiple_of(block * TILE, TILE)
                both = jnp.dot(wide[...], hits[:, pl.ds(at, TILE)], preferred_element_type=F32)
                top, rest = split(both[:cells] + both[cells:])
                to = pl.multiple_of(base + at, TILE)
                high[STRIDE : STRIDE + cells, pl.ds(to, TILE)] = top
                low[STRIDE : STRIDE + cells, pl.ds(to, TILE)] = rest
                return carry

            lax.fori_loop(0, bins // TILE, lay, 0)

        held[...] = jnp.zeros(held.shape, F32)
        needed = jnp.zeros((), F32)
        for index, which in enumerate((0, 2)):
            fields = sides(which)
            edge = float(row_count - 1) if which == 0 else 0.0
            place = 2 * lax.broadcasted_iota(jnp.int32, (pairs, 2 * slabs), 0) + (
                lax.broadcasted_iota(jnp.int32, (pairs, 2 * slabs), 1) // slabs
            )
            depth = (place if which == 0 else CAP - 1 - place) + 1
            for slab in range(2):
                charge, row, column, _ = fields[slab]
                kept = jnp.where(row == edge, charge, 0.0)
                needed = jnp.maximum(needed, jnp.max(jnp.where(kept != 0.0, depth, 0).astype(F32)))
                edges[index, slab, 0] = kept
                edges[index, slab, 1] = column
        chunks = (needed.astype(jnp.int32) + 3) // 4
        for number in range(CAP // 4):

            @pl.when(number < chunks)
            def _():
                for index, which in enumerate((0, 2)):
                    first = 4 * number if which == 0 else CAP - 4 - 4 * number
                    for slab in range(2):
                        weights = []
                        for pair in (first // 2, first // 2 + 1):
                            there = pad == edges[index, slab, 1, pair : pair + 1].astype(jnp.int32)
                            weights.append(jnp.where(there, edges[index, slab, 0, pair : pair + 1], 0.0))
                        top = jnp.concatenate(weights, axis=1)
                        rest = top - top.astype(BF16).astype(F32)
                        left = jnp.concatenate([top, rest], axis=0).astype(BF16)
                        right = jnp.concatenate(
                            [hit_rows(which, slab, first + k) for k in range(4)], axis=0
                        )
                        both = jnp.dot(left, right, preferred_element_type=F32)
                        at = bins * (1 - slab)
                        held[index, :, at : at + bins] += both[:STRIDE] + both[STRIDE:]

        for index, at in enumerate((0, STRIDE + cells)):
            top, rest = split(held[index])
            high[at : at + STRIDE] = top
            low[at : at + STRIDE] = rest

    start = pl.multiple_of(step * TILE, TILE)
    depth = table_high.shape[0]
    upper = high[:, pl.ds(start, depth)]
    shaped[...] = (
        jnp.dot(upper, table_high[...], preferred_element_type=F32)
        + jnp.dot(upper, table_low[...], preferred_element_type=F32)
        + jnp.dot(low[:, pl.ds(start, depth)], table_high[...], preferred_element_type=F32)
    )

    def spread(r, carry):
        at = pl.multiple_of(r * STRIDE, 8)
        near = [shaped[pl.ds(pl.multiple_of(at + STRIDE * a, 8), STRIDE)] for a in range(3)]
        sums = []
        for b in range(3):
            sums.append(
                response_ref[0, b] * near[0] + response_ref[1, b] * near[1] + response_ref[2, b] * near[2]
            )
        total = sums[1] + pltpu.roll(sums[0], 1, 0) + pltpu.roll(sums[2], STRIDE - 1, 0)
        out_ref[r] = total[:PPR]
        return carry

    lax.fori_loop(0, row_count, spread, 0)


def digitize(recv, shaping, response, row_count, bins):
    slabs = recv.shape[1]
    lags = shaping.shape[1]
    cells = row_count * STRIDE
    grid_rows = cells + 2 * STRIDE
    return pl.pallas_call(
        functools.partial(digitize_kernel, row_count, bins),
        out_shape=jax.ShapeDtypeStruct((row_count, PPR, bins), F32),
        grid=(bins // TILE,),
        in_specs=[
            pl.BlockSpec(memory_space=pltpu.VMEM),
            pl.BlockSpec(memory_space=pltpu.VMEM),
            pl.BlockSpec(memory_space=pltpu.SMEM),
        ],
        out_specs=pl.BlockSpec((row_count, PPR, TILE), lambda i: (0, 0, i)),
        scratch_shapes=[
            pltpu.VMEM((grid_rows, 2 * bins), BF16),
            pltpu.VMEM((grid_rows, 2 * bins), BF16),
            pltpu.VMEM((lags + TILE, TILE), BF16),
            pltpu.VMEM((lags + TILE, TILE), BF16),
            pltpu.VMEM((2 * cells, CAP * slabs), BF16),
            pltpu.VMEM((CAP * slabs, bins), BF16),
            pltpu.VMEM((8, 128), F32),
            pltpu.VMEM((grid_rows, TILE), F32),
            pltpu.VMEM((2, 2, 2, CAP // 2, 2 * slabs), F32),
            pltpu.VMEM((2, STRIDE, 2 * bins), F32),
            pltpu.VMEM((8, 128), F32),
        ],
        compiler_params=pltpu.CompilerParams(
            dimension_semantics=("arbitrary",), vmem_limit_bytes=60 * 1024 * 1024
        ),
        name="digitize",
    )(recv, shaping, response)


def solution(mesh):
    slabs, groups = mesh.shape["tm"], mesh.shape["pad"]
    row_count = PROWS // groups
    bins = 1024
    rows_y = 4 if slabs % 4 == 0 else 1

    def body(charge, pad_row, pad_column, time_bin, slab_owner, block_count, shaping, response):
        owner = slab_owner.reshape(1, slab_owner.shape[1])
        rows = route(charge, pad_row, pad_column, time_bin, owner, block_count, slabs, row_count - 1)
        received = exchange(rows, rows_y)
        return digitize(received, shaping.reshape(1, shaping.shape[0]), response, row_count, bins)

    in_specs = (P("pad", "tm"),) * 4 + (P("pad", "tm", None), P("pad", "tm"), P(), P())
    return jax.shard_map(
        body, mesh=mesh, in_specs=in_specs, out_specs=P("pad", None, "tm"), check_vma=False
    )
```

```python
import functools

import jax
import jax.numpy as jnp
from jax import lax
from jax.experimental import pallas as pl
from jax.experimental.pallas import tpu as pltpu
from jax.sharding import PartitionSpec as P

PROWS = 80
PPR = 66
STRIDE = 72
CAP = 16
FIELDS = 4
HALF = FIELDS * CAP
F32 = jnp.float32
BF16 = jnp.bfloat16
LANES = 128
TILE = 256
NT = (((1,), (1,)), ((), ()))


def split(x):
    high = x.astype(BF16)
    return high, (x - high.astype(F32)).astype(BF16)


def route_rows(last_row, slabs, charge, row, column, moment, owner, count):
    clusters = charge.shape[1]
    lane = lax.broadcasted_iota(jnp.int32, (1, clusters), 1)
    limit = jnp.zeros((1, clusters), jnp.int32)
    for block in range(clusters // LANES):
        limit = jnp.where(lane // LANES == block, count[:, block : block + 1], limit)
    live = lane % LANES < limit
    owner = jnp.where(live, owner, slabs)
    mine = owner == lax.broadcasted_iota(jnp.int32, (slabs, clusters), 0)
    upper = row == last_row
    lower = row == 0
    middle = jnp.logical_not(jnp.logical_or(upper, lower))
    kinds = [jnp.where(jnp.logical_and(mine, kind), 1.0, 0.0) for kind in (upper, middle, lower)]
    stacked = jnp.concatenate(kinds, axis=0).astype(BF16)
    earlier = (
        lax.broadcasted_iota(jnp.int32, (clusters, clusters), 0)
        < lax.broadcasted_iota(jnp.int32, (clusters, clusters), 1)
    ).astype(F32).astype(BF16)
    ranks = jnp.dot(stacked, earlier, preferred_element_type=F32)
    uppers = jnp.sum(kinds[0], axis=1, keepdims=True)
    places = (
        kinds[0] * ranks[:slabs]
        + kinds[1] * (uppers + ranks[slabs : 2 * slabs])
        + kinds[2] * ((CAP - 1) - ranks[2 * slabs :])
    )
    place = jnp.sum(places, axis=0, keepdims=True)
    slot = lax.broadcasted_iota(jnp.int32, (CAP, clusters), 0)
    half = CAP // 2
    here = place == (2 * (slot % half) + slot // half).astype(F32)
    fields = (charge, row.astype(F32), column.astype(F32), moment.astype(F32))
    spread_out = jnp.concatenate([jnp.where(here, field, 0.0) for field in fields], axis=0)
    own = lax.dot_general(
        jnp.where(mine, 1.0, 0.0), spread_out, NT, precision=lax.Precision.HIGHEST, preferred_element_type=F32
    )
    slab = lax.broadcasted_iota(jnp.int32, own.shape, 0)
    before = jnp.where(slab == 0, 0.0, pltpu.roll(own, 1, 0))
    return jnp.concatenate([own, before], axis=1)


def lag_table(shaping):
    lags = shaping.shape[1]
    line = jnp.concatenate([jnp.zeros((1, TILE), F32), shaping, jnp.zeros((1, TILE), F32)], axis=1)
    rolled = pltpu.roll(
        jnp.broadcast_to(line, (TILE, lags + 2 * TILE)), 0, 1, stride=1, stride_axis=0
    )
    blocks = []
    for block in range(lags // TILE + 1):
        at = lags + TILE - TILE * block
        blocks.append(rolled[:, at : at + TILE])
    return blocks


def zigzag(step, size):
    half = (step + 1) // 2
    away = jnp.where(step % 2 == 0, half, -half)
    return lax.rem(size // 2 + away + size, size)


def exchange_kernel(
    last_row, rows_y, rows_z, charge_ref, row_ref, column_ref, bin_ref, owner_ref, count_ref, shaping_ref,
    out_ref, table_ref, floats, ints, counts, line, rows, table, load_sem, send_sem, recv_sem, side_send, side_recv,
):
    slabs = rows.shape[0]
    groups = lax.axis_size("pad")
    me = lax.axis_index("tm")
    group = lax.axis_index("pad")
    above = lax.rem(group + 1, groups)
    below = lax.rem(group + groups - 1, groups)
    my_y, my_z = me // rows_z, lax.rem(me, rows_z)
    loads = [
        pltpu.make_async_copy(source, target, load_sem.at[index])
        for index, (source, target) in enumerate(
            (
                (charge_ref, floats),
                (row_ref, ints.at[0]),
                (column_ref, ints.at[1]),
                (bin_ref, ints.at[2]),
                (owner_ref, ints.at[3]),
                (count_ref, counts),
                (shaping_ref, line),
            )
        )
    ]
    for load in loads:
        load.start()

    def peer_of(step):
        z = lax.rem(my_z + zigzag(step // rows_y, rows_z), rows_z)
        y = lax.rem(my_y + zigzag(lax.rem(step, rows_y), rows_y), rows_y)
        return y * rows_z + z

    barrier = pltpu.get_barrier_semaphore()

    def greet(step, carry):
        pl.semaphore_signal(
            barrier, inc=1, device_id=(peer_of(step), group), device_id_type=pl.DeviceIdType.MESH
        )
        return carry

    lax.fori_loop(0, slabs - 1, greet, 0)
    for side in (above, below):
        pl.semaphore_signal(barrier, inc=1, device_id=(me, side), device_id_type=pl.DeviceIdType.MESH)
    for load in loads:
        load.wait()
    rows[...] = route_rows(
        last_row, slabs, floats[...], ints[0], ints[1], ints[2], ints[3], counts[...]
    )
    for index, block in enumerate(lag_table(line[...])):
        high, low = split(block)
        table[0, TILE * index : TILE * (index + 1)] = high
        table[1, TILE * index : TILE * (index + 1)] = low
    store = pltpu.make_async_copy(table, table_ref, load_sem.at[0])
    store.start()
    out_ref[1, pl.ds(me, 1)] = rows[pl.ds(me, 1)]
    pl.semaphore_wait(barrier, slabs + 1)

    def send(step, carry):
        peer = peer_of(step)
        pltpu.make_async_remote_copy(
            src_ref=rows.at[pl.ds(peer, 1)],
            dst_ref=out_ref.at[1, pl.ds(me, 1)],
            send_sem=send_sem,
            recv_sem=recv_sem,
            device_id=(peer, group),
            device_id_type=pl.DeviceIdType.MESH,
        ).start()
        return carry

    lax.fori_loop(0, slabs - 1, send, 0)
    some = rows.at[pl.ds(0, slabs - 1)]
    pltpu.make_async_copy(some, out_ref.at[1, pl.ds(0, slabs - 1)], recv_sem).wait()
    copies = []
    for index, (side, place) in enumerate(((above, 0), (below, 2))):
        copies.append(
            pltpu.make_async_remote_copy(
                src_ref=out_ref.at[1],
                dst_ref=out_ref.at[place],
                send_sem=side_send.at[index],
                recv_sem=side_recv.at[index],
                device_id=(me, side),
                device_id_type=pl.DeviceIdType.MESH,
            )
        )
        copies[-1].start()
    pltpu.make_async_copy(some, out_ref.at[1, pl.ds(0, slabs - 1)], send_sem).wait()
    store.wait()
    for copy in copies:
        copy.wait()

    @pl.when(group == 0)
    def _():
        out_ref[0] = jnp.zeros(out_ref.shape[1:], F32)

    @pl.when(group == groups - 1)
    def _():
        out_ref[2] = jnp.zeros(out_ref.shape[1:], F32)


def exchange(charge, row, column, moment, owner, count, shaping, slabs, last_row, rows_y):
    clusters, lags = charge.shape[1], shaping.shape[1]
    return pl.pallas_call(
        functools.partial(exchange_kernel, last_row, rows_y, slabs // rows_y),
        out_shape=(
            jax.ShapeDtypeStruct((3, slabs, 2 * HALF), F32),
            jax.ShapeDtypeStruct((2, lags + TILE, TILE), BF16),
        ),
        in_specs=[pl.BlockSpec(memory_space=pl.ANY)] * 7,
        out_specs=(pl.BlockSpec(memory_space=pltpu.VMEM), pl.BlockSpec(memory_space=pl.ANY)),
        scratch_shapes=[
            pltpu.VMEM((1, clusters), F32),
            pltpu.VMEM((4, 1, clusters), jnp.int32),
            pltpu.VMEM(count.shape, jnp.int32),
            pltpu.VMEM((1, lags), F32),
            pltpu.VMEM((slabs, 2 * HALF), F32),
            pltpu.VMEM((2, lags + TILE, TILE), BF16),
            pltpu.SemaphoreType.DMA((7,)),
            pltpu.SemaphoreType.DMA,
            pltpu.SemaphoreType.DMA,
            pltpu.SemaphoreType.DMA((2,)),
            pltpu.SemaphoreType.DMA((2,)),
        ],
        compiler_params=pltpu.CompilerParams(collective_id=0, has_side_effects=True),
        name="exchange",
    )(charge, row, column, moment, owner, count, shaping)


def digitize_kernel(
    row_count, bins, recv_ref, table_ref, response_ref, out_ref,
    high, low, table, wides, hits, shaped, edges, held, staged, table_sem, out_sem,
):
    load = pltpu.make_async_copy(table_ref, table, table_sem)
    load.start()
    slabs = recv_ref.shape[1]
    cells = row_count * STRIDE
    pairs = CAP // 2

    def sides(which):
        flipped = jnp.transpose(recv_ref[which])
        return [
            [
                jnp.concatenate(
                    [
                        flipped[HALF * slab + CAP * field : HALF * slab + CAP * field + pairs],
                        flipped[HALF * slab + CAP * field + pairs : HALF * slab + CAP * (field + 1)],
                    ],
                    axis=1,
                )
                for field in range(FIELDS)
            ]
            for slab in range(2)
        ]

    def hit_rows(which, slab, slot):
        at = HALF * slab + CAP * 3 + (slot % 2) * pairs + slot // 2
        column = recv_ref[which, :, at : at + 1].astype(jnp.int32)
        moment = lax.broadcasted_iota(jnp.int32, (slabs, bins), 1)
        return jnp.where(moment == column, 1.0, 0.0).astype(BF16)

    own = sides(1)
    pad = lax.broadcasted_iota(jnp.int32, (STRIDE, 2 * slabs), 0)
    for slab in range(2):
        charge, row, column, _ = own[slab]
        wide = wides.at[slab]
        for pair in range(pairs):
            there = pad == column[pair : pair + 1].astype(jnp.int32)
            lanes = slice(2 * slabs * pair, 2 * slabs * (pair + 1))
            for lead in range(0, row_count, 2):
                both = []
                for r in (lead, lead + 1):
                    value = jnp.where(row[pair : pair + 1] == float(r), charge[pair : pair + 1], 0.0)
                    both.append(jnp.where(there, value, 0.0))
                top, rest = split(jnp.concatenate(both, axis=0))
                at = lead * STRIDE
                wide[at : at + 2 * STRIDE, lanes] = top
                wide[cells + at : cells + at + 2 * STRIDE, lanes] = rest
        for slot in range(CAP):
            hits[slab, slabs * slot : slabs * (slot + 1)] = hit_rows(1, slab, slot)
        base = bins * (1 - slab)
        both = jnp.dot(wide[...], hits[slab], preferred_element_type=F32)
        top, rest = split(both[:cells] + both[cells:])
        high[STRIDE : STRIDE + cells, base : base + bins] = top
        low[STRIDE : STRIDE + cells, base : base + bins] = rest

    held[...] = jnp.zeros(held.shape, F32)
    needed = jnp.zeros((), F32)
    for index, which in enumerate((0, 2)):
        fields = sides(which)
        edge = float(row_count - 1) if which == 0 else 0.0
        place = 2 * lax.broadcasted_iota(jnp.int32, (pairs, 2 * slabs), 0) + (
            lax.broadcasted_iota(jnp.int32, (pairs, 2 * slabs), 1) // slabs
        )
        depth = (place if which == 0 else CAP - 1 - place) + 1
        for slab in range(2):
            charge, row, column, _ = fields[slab]
            kept = jnp.where(row == edge, charge, 0.0)
            needed = jnp.maximum(needed, jnp.max(jnp.where(kept != 0.0, depth, 0).astype(F32)))
            edges[index, slab, 0] = kept
            edges[index, slab, 1] = column
    chunks = (needed.astype(jnp.int32) + 3) // 4
    for number in range(CAP // 4):

        @pl.when(number < chunks)
        def _():
            for index, which in enumerate((0, 2)):
                first = 4 * number if which == 0 else CAP - 4 - 4 * number
                for slab in range(2):
                    weights = []
                    for pair in (first // 2, first // 2 + 1):
                        there = pad == edges[index, slab, 1, pair : pair + 1].astype(jnp.int32)
                        weights.append(jnp.where(there, edges[index, slab, 0, pair : pair + 1], 0.0))
                    top = jnp.concatenate(weights, axis=1)
                    rest = top - top.astype(BF16).astype(F32)
                    left = jnp.concatenate([top, rest], axis=0).astype(BF16)
                    right = jnp.concatenate(
                        [hit_rows(which, slab, first + k) for k in range(4)], axis=0
                    )
                    both = jnp.dot(left, right, preferred_element_type=F32)
                    at = bins * (1 - slab)
                    held[index, :, at : at + bins] += both[:STRIDE] + both[STRIDE:]

    for index, at in enumerate((0, STRIDE + cells)):
        top, rest = split(held[index])
        high[at : at + STRIDE] = top
        low[at : at + STRIDE] = rest

    load.wait()
    depth = table.shape[1]
    steps = bins // TILE
    copies = []
    for step in range(steps + 1):
        if step < steps:
            upper = high[:, TILE * step : TILE * step + depth]
            shaped[step % 2] = (
                jnp.dot(upper, table[0], preferred_element_type=F32)
                + jnp.dot(upper, table[1], preferred_element_type=F32)
                + jnp.dot(
                    low[:, TILE * step : TILE * step + depth], table[0], preferred_element_type=F32
                )
            )
        if step > 0:
            done = step - 1
            if done >= 2:
                copies[done - 2].wait()
            for r in range(row_count):
                near = [shaped[done % 2, STRIDE * (r + a) : STRIDE * (r + a + 1)] for a in range(3)]
                sums = []
                for b in range(3):
                    sums.append(
                        response_ref[0, b] * near[0] + response_ref[1, b] * near[1] + response_ref[2, b] * near[2]
                    )
                total = sums[1] + pltpu.roll(sums[0], 1, 0) + pltpu.roll(sums[2], STRIDE - 1, 0)
                staged[done % 2, r] = total[:PPR]
            copies.append(
                pltpu.make_async_copy(
                    staged.at[done % 2],
                    out_ref.at[:, :, pl.ds(TILE * done, TILE)],
                    out_sem.at[done % 2],
                )
            )
            copies[-1].start()
    for copy in copies[-2:]:
        copy.wait()


def digitize(recv, table, response, row_count, bins):
    slabs = recv.shape[1]
    cells = row_count * STRIDE
    grid_rows = cells + 2 * STRIDE
    return pl.pallas_call(
        functools.partial(digitize_kernel, row_count, bins),
        out_shape=jax.ShapeDtypeStruct((row_count, PPR, bins), F32),
        in_specs=[
            pl.BlockSpec(memory_space=pltpu.VMEM),
            pl.BlockSpec(memory_space=pl.ANY),
            pl.BlockSpec(memory_space=pltpu.SMEM),
        ],
        out_specs=pl.BlockSpec(memory_space=pl.ANY),
        scratch_shapes=[
            pltpu.VMEM((grid_rows, 2 * bins), BF16),
            pltpu.VMEM((grid_rows, 2 * bins), BF16),
            pltpu.VMEM(table.shape, BF16),
            pltpu.VMEM((2, 2 * cells, CAP * slabs), BF16),
            pltpu.VMEM((2, CAP * slabs, bins), BF16),
            pltpu.VMEM((2, grid_rows, TILE), F32),
            pltpu.VMEM((2, 2, 2, CAP // 2, 2 * slabs), F32),
            pltpu.VMEM((2, STRIDE, 2 * bins), F32),
            pltpu.VMEM((2, row_count, PPR, TILE), F32),
            pltpu.SemaphoreType.DMA,
            pltpu.SemaphoreType.DMA((2,)),
        ],
        compiler_params=pltpu.CompilerParams(vmem_limit_bytes=60 * 1024 * 1024),
        name="digitize",
    )(recv, table, response)


def solution(mesh):
    slabs, groups = mesh.shape["tm"], mesh.shape["pad"]
    row_count = PROWS // groups
    bins = 1024
    rows_y = 4 if slabs % 4 == 0 else 1

    def body(charge, pad_row, pad_column, time_bin, slab_owner, block_count, shaping, response):
        owner = slab_owner.reshape(1, slab_owner.shape[1])
        line = shaping.reshape(1, shaping.shape[0])
        received, table = exchange(
            charge, pad_row, pad_column, time_bin, owner, block_count, line, slabs, row_count - 1, rows_y
        )
        return digitize(received, table, response, row_count, bins)

    in_specs = (P("pad", "tm"),) * 4 + (P("pad", "tm", None), P("pad", "tm"), P(), P())
    return jax.shard_map(
        body, mesh=mesh, in_specs=in_specs, out_specs=P("pad", None, "tm"), check_vma=False
    )
```

```python
import functools

import jax
import jax.numpy as jnp
from jax import lax
from jax.experimental import pallas as pl
from jax.experimental.pallas import tpu as pltpu
from jax.sharding import PartitionSpec as P

PROWS = 80
PPR = 66
STRIDE = 72
CAP = 16
FIELDS = 4
HALF = FIELDS * CAP
F32 = jnp.float32
BF16 = jnp.bfloat16
F8 = jnp.float8_e4m3fn
GRID, GRID_LOW = 2.0**-3, 2.0**8
TABLE_HIGH, TABLE_LOW = 2.0**7, 2.0**15
CHARGE_LOW = 2.0**17
UPPER = 448
MAIN = 12
FINE = 2.0**-15
LANES = 128
TILE = 256
NT = (((1,), (1,)), ((), ()))


def split(x):
    high = x.astype(BF16)
    return high, (x - high.astype(F32)).astype(BF16)


def route_rows(last_row, slabs, charge, row, column, moment, owner, count):
    clusters = charge.shape[1]
    lane = lax.broadcasted_iota(jnp.int32, (1, clusters), 1)
    limit = jnp.zeros((1, clusters), jnp.int32)
    for block in range(clusters // LANES):
        limit = jnp.where(lane // LANES == block, count[:, block : block + 1], limit)
    live = lane % LANES < limit
    owner = jnp.where(live, owner, slabs)
    mine = owner == lax.broadcasted_iota(jnp.int32, (slabs, clusters), 0)
    middle = (last_row + 1) // 2
    order = (
        row == last_row,
        jnp.logical_and(row >= middle, row < last_row),
        jnp.logical_and(row < middle, row > 0),
        row == 0,
    )
    kinds = [jnp.where(jnp.logical_and(mine, kind), 1.0, 0.0) for kind in order]
    stacked = jnp.concatenate(kinds, axis=0).astype(BF16)
    earlier = (
        lax.broadcasted_iota(jnp.int32, (clusters, clusters), 0)
        < lax.broadcasted_iota(jnp.int32, (clusters, clusters), 1)
    ).astype(F32).astype(BF16)
    ranks = jnp.dot(stacked, earlier, preferred_element_type=F32)
    ranks = [ranks[slabs * k : slabs * (k + 1)] for k in range(4)]
    firsts = jnp.sum(kinds[0], axis=1, keepdims=True)
    lasts = jnp.sum(kinds[3], axis=1, keepdims=True)
    places = (
        kinds[0] * ranks[0]
        + kinds[1] * (firsts + ranks[1])
        + kinds[2] * ((CAP - 1) - lasts - ranks[2])
        + kinds[3] * ((CAP - 1) - ranks[3])
    )
    place = jnp.sum(places, axis=0, keepdims=True)
    slot = lax.broadcasted_iota(jnp.int32, (CAP, clusters), 0)
    half = CAP // 2
    here = place == (2 * (slot % half) + slot // half).astype(F32)
    fields = (charge, row.astype(F32), column.astype(F32), moment.astype(F32))
    spread_out = jnp.concatenate([jnp.where(here, field, 0.0) for field in fields], axis=0)
    own = lax.dot_general(
        jnp.where(mine, 1.0, 0.0), spread_out, NT, precision=lax.Precision.HIGHEST, preferred_element_type=F32
    )
    slab = lax.broadcasted_iota(jnp.int32, own.shape, 0)
    before = jnp.where(slab == 0, 0.0, pltpu.roll(own, 1, 0))
    return jnp.concatenate([own, before], axis=1)


def lag_table(shaping):
    lags = shaping.shape[1]
    line = jnp.concatenate([jnp.zeros((1, TILE), F32), shaping, jnp.zeros((1, TILE), F32)], axis=1)
    rolled = pltpu.roll(
        jnp.broadcast_to(line, (TILE, lags + 2 * TILE)), 0, 1, stride=1, stride_axis=0
    )
    blocks = []
    for block in range(lags // TILE + 1):
        at = lags + TILE - TILE * block
        blocks.append(rolled[:, at : at + TILE])
    return blocks


def in_hbm(x):
    return pltpu.with_memory_space_constraint(x, pltpu.HBM)


def zigzag(step, size):
    half = (step + 1) // 2
    away = jnp.where(step % 2 == 0, half, -half)
    return lax.rem(size // 2 + away + size, size)


def exchange_kernel(
    last_row, rows_y, rows_z, charge_ref, row_ref, column_ref, bin_ref, owner_ref, count_ref, shaping_ref,
    out_ref, table_ref, floats, ints, counts, line, rows, table, load_sem, send_sem, recv_sem, side_send, side_recv,
):
    slabs = rows.shape[0]
    groups = lax.axis_size("pad")
    me = lax.axis_index("tm")
    group = lax.axis_index("pad")
    above = lax.rem(group + 1, groups)
    below = lax.rem(group + groups - 1, groups)
    my_y, my_z = me // rows_z, lax.rem(me, rows_z)
    loads = [
        pltpu.make_async_copy(source, target, load_sem.at[index])
        for index, (source, target) in enumerate(
            (
                (charge_ref, floats),
                (row_ref, ints.at[0]),
                (column_ref, ints.at[1]),
                (bin_ref, ints.at[2]),
                (owner_ref, ints.at[3]),
                (count_ref, counts),
                (shaping_ref, line),
            )
        )
    ]
    for load in loads:
        load.start()

    def peer_of(step):
        z = lax.rem(my_z + zigzag(step // rows_y, rows_z), rows_z)
        y = lax.rem(my_y + zigzag(lax.rem(step, rows_y), rows_y), rows_y)
        return y * rows_z + z

    barrier = pltpu.get_barrier_semaphore()

    def greet(step, carry):
        pl.semaphore_signal(
            barrier, inc=1, device_id=(peer_of(step), group), device_id_type=pl.DeviceIdType.MESH
        )
        return carry

    lax.fori_loop(0, slabs - 1, greet, 0)
    for side in (above, below):
        pl.semaphore_signal(barrier, inc=1, device_id=(me, side), device_id_type=pl.DeviceIdType.MESH)
    for load in loads:
        load.wait()
    rows[...] = route_rows(
        last_row, slabs, floats[...], ints[0], ints[1], ints[2], ints[3], counts[...]
    )
    for index, block in enumerate(lag_table(line[...])):
        high, low = split(block)
        table[0, TILE * index : TILE * (index + 1)] = high
        table[1, TILE * index : TILE * (index + 1)] = low
    store = pltpu.make_async_copy(table, table_ref, load_sem.at[0])
    store.start()
    out_ref[1, pl.ds(me, 1)] = rows[pl.ds(me, 1)]
    pl.semaphore_wait(barrier, slabs + 1)

    def send(step, carry):
        peer = peer_of(step)
        pltpu.make_async_remote_copy(
            src_ref=rows.at[pl.ds(peer, 1)],
            dst_ref=out_ref.at[1, pl.ds(me, 1)],
            send_sem=send_sem,
            recv_sem=recv_sem,
            device_id=(peer, group),
            device_id_type=pl.DeviceIdType.MESH,
        ).start()
        return carry

    lax.fori_loop(0, slabs - 1, send, 0)
    some = rows.at[pl.ds(0, slabs - 1)]
    pltpu.make_async_copy(some, out_ref.at[1, pl.ds(0, slabs - 1)], recv_sem).wait()
    copies = []
    for index, (side, place) in enumerate(((above, 0), (below, 2))):
        copies.append(
            pltpu.make_async_remote_copy(
                src_ref=out_ref.at[1],
                dst_ref=out_ref.at[place],
                send_sem=side_send.at[index],
                recv_sem=side_recv.at[index],
                device_id=(me, side),
                device_id_type=pl.DeviceIdType.MESH,
            )
        )
        copies[-1].start()
    pltpu.make_async_copy(some, out_ref.at[1, pl.ds(0, slabs - 1)], send_sem).wait()
    store.wait()
    for copy in copies:
        copy.wait()

    @pl.when(group == 0)
    def _():
        out_ref[0] = jnp.zeros(out_ref.shape[1:], F32)

    @pl.when(group == groups - 1)
    def _():
        out_ref[2] = jnp.zeros(out_ref.shape[1:], F32)


def exchange(charge, row, column, moment, owner, count, shaping, slabs, last_row, rows_y):
    clusters, lags = charge.shape[1], shaping.shape[1]
    return pl.pallas_call(
        functools.partial(exchange_kernel, last_row, rows_y, slabs // rows_y),
        out_shape=(
            jax.ShapeDtypeStruct((3, slabs, 2 * HALF), F32),
            jax.ShapeDtypeStruct((2, lags + TILE, TILE), BF16),
        ),
        in_specs=[pl.BlockSpec(memory_space=pltpu.HBM)] * 7,
        out_specs=(pl.BlockSpec(memory_space=pltpu.VMEM), pl.BlockSpec(memory_space=pl.ANY)),
        scratch_shapes=[
            pltpu.VMEM((1, clusters), F32),
            pltpu.VMEM((4, 1, clusters), jnp.int32),
            pltpu.VMEM(count.shape, jnp.int32),
            pltpu.VMEM((1, lags), F32),
            pltpu.VMEM((slabs, 2 * HALF), F32),
            pltpu.VMEM((2, lags + TILE, TILE), BF16),
            pltpu.SemaphoreType.DMA((7,)),
            pltpu.SemaphoreType.DMA,
            pltpu.SemaphoreType.DMA,
            pltpu.SemaphoreType.DMA((2,)),
            pltpu.SemaphoreType.DMA((2,)),
        ],
        compiler_params=pltpu.CompilerParams(
            collective_id=0, has_side_effects=True, vmem_limit_bytes=16 * 1024 * 1024
        ),
        name="exchange",
    )(*(in_hbm(x) for x in (charge, row, column, moment, owner, count, shaping)))


def digitize_kernel(
    row_count, bins, recv_ref, table_ref, weights_ref, out_ref,
    high, high8, low8, table, table8, wides, wides8, hits, hits8, shaped, owns, edges, held, staged, response_ref, table_sem, weights_sem, out_sem,
):
    fetch = pltpu.make_async_copy(weights_ref, response_ref, weights_sem)
    fetch.start()
    load = pltpu.make_async_copy(table_ref, table, table_sem)
    load.start()
    slabs = recv_ref.shape[1]
    cells = row_count * STRIDE
    pairs = CAP // 2

    def sides(which):
        flipped = jnp.transpose(recv_ref[which])
        return [
            [
                jnp.concatenate(
                    [
                        flipped[HALF * slab + CAP * field : HALF * slab + CAP * field + pairs],
                        flipped[HALF * slab + CAP * field + pairs : HALF * slab + CAP * (field + 1)],
                    ],
                    axis=1,
                )
                for field in range(FIELDS)
            ]
            for slab in range(2)
        ]

    lane = lax.broadcasted_iota(jnp.int32, (slabs, LANES), 1).astype(F32)

    def digits(which, slab):
        at = HALF * slab + CAP * 3
        moment = recv_ref[which, :, at : at + CAP]
        block = jnp.floor(moment * (1.0 / LANES))
        return block, moment - LANES * block

    def hit_rows(digit, slot):
        at = (slot % 2) * pairs + slot // 2
        block, inner = (jnp.broadcast_to(d[:, at : at + 1], (slabs, LANES)) for d in digit)
        row = jnp.where(inner == lane, 1.0, 0.0).astype(BF16)
        block = block.astype(BF16)
        zero = jnp.zeros((slabs, LANES), BF16)
        return [jnp.where(block == float(k), row, zero) for k in range(bins // LANES)]

    def keep(at, grid, to, width):
        top = grid.astype(BF16)
        there = pl.ds(at, grid.shape[0]), pl.ds(to, width)
        high[there] = top
        high8[there] = grid.astype(F8)
        low8[there] = ((grid - top.astype(F32)) * GRID_LOW).astype(F8)

    half_rows = row_count // 2
    half_cells = half_rows * STRIDE
    bases = (0, UPPER)
    pad = lax.broadcasted_iota(jnp.int32, (STRIDE, 2 * slabs), 0)
    charges, rows_of, columns_of = [], [], []
    place = 2 * lax.broadcasted_iota(jnp.int32, (pairs, 2 * slabs), 0) + (
        lax.broadcasted_iota(jnp.int32, (pairs, 2 * slabs), 1) // slabs
    )
    spill = jnp.zeros((pairs, 2 * slabs), F32)
    for fields in sides(1):
        charge, row, column, _ = fields
        charges.append(charge * GRID)
        rows_of.append(row)
        columns_of.append(column)
        slab = len(charges) - 1
        for index, field in enumerate((charges[-1], row, column)):
            owns[slab, index] = field
        outside = jnp.where(row < float(half_rows), CAP - MAIN - place, place - MAIN + 1)
        spill = jnp.where(jnp.logical_and(charge != 0.0, outside > 0), 1.0, spill)

    def fill(slab, half, which, lines_of):
        for pair in which:
            charge, row, column = lines_of(pair)
            first = half_rows * half if isinstance(half, int) else (half_rows * half).astype(F32)
            top = charge.astype(BF16).astype(F32)
            rest = (charge - top) * CHARGE_LOW
            lanes = pl.ds(pl.multiple_of(2 * slabs * pair, 2 * slabs), 2 * slabs)
            for lead in range(0, half_rows, 4):
                count = min(4, half_rows - lead)
                size = count * STRIDE
                pads = jnp.concatenate([pad] * count, axis=0).astype(F32).astype(BF16)
                there = pads == jnp.broadcast_to(column, (size, 2 * slabs)).astype(BF16)
                blank = jnp.zeros((size, 2 * slabs), BF16)
                for part, target in ((top, wides), (rest, wides8)):
                    lines = []
                    for r in range(lead, lead + count):
                        value = jnp.where(row == first + float(r), part, 0.0)
                        lines.append(jnp.broadcast_to(value, (STRIDE, 2 * slabs)))
                    values = jnp.concatenate(lines, axis=0).astype(BF16)
                    target[slab, half, lead * STRIDE : lead * STRIDE + size, lanes] = jnp.where(
                        there, values, blank
                    ).astype(target.dtype)

    def lay(slab, half, begin, end):
        inner = slice(begin * slabs, end * slabs)
        grid = jnp.dot(wides[slab, half, :, inner], hits[slab, inner], preferred_element_type=F32)
        grid += (1.0 / CHARGE_LOW) * jnp.dot(
            wides8[slab, half, :, inner], hits8[slab, inner], preferred_element_type=F32
        )
        base = bases[half] if isinstance(half, int) else pl.multiple_of(UPPER * half, UPPER)
        to = bins * (1 - slab) if isinstance(slab, int) else pl.multiple_of(bins * (1 - slab), bins)
        keep(base, grid, to, bins)

    for slab in range(2):
        digit = digits(1, slab)
        for slot in range(CAP):
            for k, piece in enumerate(hit_rows(digit, slot)):
                there = slice(slabs * slot, slabs * (slot + 1))
                hits[slab, there, LANES * k : LANES * (k + 1)] = piece
                hits8[slab, there, LANES * k : LANES * (k + 1)] = piece.astype(F8)
        for half, begin in ((0, CAP - MAIN), (1, 0)):
            fill(
                slab,
                half,
                range(begin // 2, (begin + MAIN) // 2),
                lambda pair: [f[slab][pair : pair + 1] for f in (charges, rows_of, columns_of)],
            )
            lay(slab, half, begin, begin + MAIN)

    @pl.when(jnp.max(spill) > 0.0)
    def _():
        def again(index, carry):
            slab, half = index // 2, index % 2
            rest = (CAP - MAIN) // 2
            pair = (pairs - rest) * half
            fill(
                slab,
                half,
                [pair + k for k in range(rest)],
                lambda pair: [owns[slab, k, pl.ds(pair, 1)] for k in range(3)],
            )
            lay(slab, half, 0, CAP)
            return carry

        lax.fori_loop(0, 4, again, 0)

    held[...] = jnp.zeros(held.shape, F32)
    needed = jnp.zeros((), F32)
    for index, which in enumerate((0, 2)):
        fields = sides(which)
        edge = float(row_count - 1) if which == 0 else 0.0
        depth = (place if which == 0 else CAP - 1 - place) + 1
        for slab in range(2):
            charge, row, column, _ = fields[slab]
            kept = jnp.where(row == edge, charge * GRID, 0.0)
            needed = jnp.maximum(needed, jnp.max(jnp.where(kept != 0.0, depth, 0).astype(F32)))
            edges[index, slab, 0] = kept
            edges[index, slab, 1] = column
    chunks = (needed.astype(jnp.int32) + 3) // 4
    for number in range(CAP // 4):

        @pl.when(number < chunks)
        def _():
            for index, which in enumerate((0, 2)):
                first = 4 * number if which == 0 else CAP - 4 - 4 * number
                for slab in range(2):
                    weights = []
                    for pair in (first // 2, first // 2 + 1):
                        there = pad == edges[index, slab, 1, pair : pair + 1].astype(jnp.int32)
                        weights.append(jnp.where(there, edges[index, slab, 0, pair : pair + 1], 0.0))
                    top = jnp.concatenate(weights, axis=1)
                    rest = top - top.astype(BF16).astype(F32)
                    left = jnp.concatenate([top, rest], axis=0).astype(BF16)
                    digit = digits(which, slab)
                    right = jnp.concatenate(
                        [jnp.concatenate(hit_rows(digit, first + k), axis=1) for k in range(4)], axis=0
                    )
                    both = jnp.dot(left, right, preferred_element_type=F32)
                    at = bins * (1 - slab)
                    held[index, :, at : at + bins] += both[:STRIDE] + both[STRIDE:]

    for index in range(2):
        keep(bases[index] + half_cells, held[index], 0, 2 * bins)

    load.wait()
    table8[0] = (table[0].astype(F32) * TABLE_HIGH).astype(F8)
    table8[1] = (table[1].astype(F32) * TABLE_LOW).astype(F8)
    depth = table.shape[1]
    steps = bins // TILE
    fetch.wait()
    weights = [[response_ref[a, b] * (1.0 / GRID) for b in range(3)] for a in range(3)]
    copies = []
    for step in range(steps + 1):
        if step < steps:
            near = slice(TILE * step, TILE * step + depth)
            fine = jnp.dot(
                jnp.concatenate([low8[:, near], high8[:, near]], axis=1),
                table8[...].reshape(2 * depth, TILE),
                preferred_element_type=F32,
            )
            shaped[step % 2] = jnp.dot(high[:, near], table[0], preferred_element_type=F32) + FINE * fine
        if step > 0:
            done = step - 1
            if done >= 2:
                copies[done - 2].wait()
            for r in range(row_count):
                near = []
                for a in range(3):
                    at = r + a - 1
                    at = half_rows if at < 0 else at
                    at = at * STRIDE if r + a <= half_rows else UPPER + (at - half_rows) * STRIDE
                    near.append(shaped[done % 2, at : at + STRIDE])
                sums = []
                for b in range(3):
                    sums.append(
                        weights[0][b] * near[0] + weights[1][b] * near[1] + weights[2][b] * near[2]
                    )
                total = sums[1] + pltpu.roll(sums[0], 1, 0) + pltpu.roll(sums[2], STRIDE - 1, 0)
                staged[done % 2, r] = total[:PPR]
            copies.append(
                pltpu.make_async_copy(
                    staged.at[done % 2],
                    out_ref.at[:, :, pl.ds(TILE * done, TILE)],
                    out_sem.at[done % 2],
                )
            )
            copies[-1].start()
    for copy in copies[-2:]:
        copy.wait()


def digitize(recv, table, response, row_count, bins):
    slabs = recv.shape[1]
    cells = row_count * STRIDE
    grid_rows = UPPER + cells // 2 + STRIDE
    return pl.pallas_call(
        functools.partial(digitize_kernel, row_count, bins),
        out_shape=jax.ShapeDtypeStruct((row_count, PPR, bins), F32),
        in_specs=[
            pl.BlockSpec(memory_space=pltpu.VMEM),
            pl.BlockSpec(memory_space=pl.ANY),
            pl.BlockSpec(memory_space=pltpu.HBM),
        ],
        out_specs=pl.BlockSpec(memory_space=pl.ANY),
        scratch_shapes=[
            pltpu.VMEM((grid_rows, 2 * bins), BF16),
            pltpu.VMEM((grid_rows, 2 * bins), F8),
            pltpu.VMEM((grid_rows, 2 * bins), F8),
            pltpu.VMEM(table.shape, BF16),
            pltpu.VMEM(table.shape, F8),
            pltpu.VMEM((2, 2, cells // 2, CAP * slabs), BF16),
            pltpu.VMEM((2, 2, cells // 2, CAP * slabs), F8),
            pltpu.VMEM((2, CAP * slabs, bins), BF16),
            pltpu.VMEM((2, CAP * slabs, bins), F8),
            pltpu.VMEM((2, grid_rows, TILE), F32),
            pltpu.VMEM((2, 3, CAP // 2, 2 * slabs), F32),
            pltpu.VMEM((2, 2, 2, CAP // 2, 2 * slabs), F32),
            pltpu.VMEM((2, STRIDE, 2 * bins), F32),
            pltpu.VMEM((2, row_count, PPR, TILE), F32),
            pltpu.SMEM(response.shape, F32),
            pltpu.SemaphoreType.DMA,
            pltpu.SemaphoreType.DMA,
            pltpu.SemaphoreType.DMA((2,)),
        ],
        compiler_params=pltpu.CompilerParams(vmem_limit_bytes=40 * 1024 * 1024),
        name="digitize",
    )(recv, table, in_hbm(response))


def solution(mesh):
    slabs, groups = mesh.shape["tm"], mesh.shape["pad"]
    row_count = PROWS // groups
    bins = 1024
    rows_y = 4 if slabs % 4 == 0 else 1

    def body(charge, pad_row, pad_column, time_bin, slab_owner, block_count, shaping, response):
        owner = slab_owner.reshape(1, slab_owner.shape[1])
        line = shaping.reshape(1, shaping.shape[0])
        received, table = exchange(
            charge, pad_row, pad_column, time_bin, owner, block_count, line, slabs, row_count - 1, rows_y
        )
        return digitize(received, table, response, row_count, bins)

    in_specs = (P("pad", "tm"),) * 4 + (P("pad", "tm", None), P("pad", "tm"), P(), P())
    return jax.shard_map(
        body, mesh=mesh, in_specs=in_specs, out_specs=P("pad", None, "tm"), check_vma=False
    )
```

```python
import functools

import jax
import jax.numpy as jnp
from jax import lax
from jax.experimental import pallas as pl
from jax.experimental.pallas import tpu as pltpu
from jax.sharding import PartitionSpec as P

PROWS = 80
PPR = 66
STRIDE = 72
CAP = 16
FIELDS = 4
HALF = FIELDS * CAP
F32 = jnp.float32
BF16 = jnp.bfloat16
F8 = jnp.float8_e4m3fn
GRID, GRID_LOW = 2.0**-3, 2.0**8
TABLE_HIGH, TABLE_LOW = 2.0**7, 2.0**15
CHARGE_LOW = 2.0**17
FINE = 2.0**-15
LANES = 128
TILE = 256
NT = (((1,), (1,)), ((), ()))


def split(x):
    high = x.astype(BF16)
    return high, (x - high.astype(F32)).astype(BF16)


def route_rows(last_row, slabs, charge, row, column, moment, owner, count):
    clusters = charge.shape[1]
    lane = lax.broadcasted_iota(jnp.int32, (1, clusters), 1)
    limit = jnp.zeros((1, clusters), jnp.int32)
    for block in range(clusters // LANES):
        limit = jnp.where(lane // LANES == block, count[:, block : block + 1], limit)
    live = lane % LANES < limit
    owner = jnp.where(live, owner, slabs)
    mine = owner == lax.broadcasted_iota(jnp.int32, (slabs, clusters), 0)
    middle = (last_row + 1) // 2
    order = (
        row == last_row,
        jnp.logical_and(row >= middle, row < last_row),
        jnp.logical_and(row < middle, row > 0),
        row == 0,
    )
    kinds = [jnp.where(jnp.logical_and(mine, kind), 1.0, 0.0) for kind in order]
    stacked = jnp.concatenate(kinds, axis=0).astype(BF16)
    earlier = (
        lax.broadcasted_iota(jnp.int32, (clusters, clusters), 0)
        < lax.broadcasted_iota(jnp.int32, (clusters, clusters), 1)
    ).astype(F32).astype(BF16)
    ranks = jnp.dot(stacked, earlier, preferred_element_type=F32)
    ranks = [ranks[slabs * k : slabs * (k + 1)] for k in range(4)]
    firsts = jnp.sum(kinds[0], axis=1, keepdims=True)
    lasts = jnp.sum(kinds[3], axis=1, keepdims=True)
    places = (
        kinds[0] * ranks[0]
        + kinds[1] * (firsts + ranks[1])
        + kinds[2] * ((CAP - 1) - lasts - ranks[2])
        + kinds[3] * ((CAP - 1) - ranks[3])
    )
    place = jnp.sum(places, axis=0, keepdims=True)
    slot = lax.broadcasted_iota(jnp.int32, (CAP, clusters), 0)
    half = CAP // 2
    here = place == (2 * (slot % half) + slot // half).astype(F32)
    fields = (charge, row.astype(F32), column.astype(F32), moment.astype(F32))
    spread_out = jnp.concatenate([jnp.where(here, field, 0.0) for field in fields], axis=0)
    own = lax.dot_general(
        jnp.where(mine, 1.0, 0.0), spread_out, NT, precision=lax.Precision.HIGHEST, preferred_element_type=F32
    )
    slab = lax.broadcasted_iota(jnp.int32, own.shape, 0)
    before = jnp.where(slab == 0, 0.0, pltpu.roll(own, 1, 0))
    return jnp.concatenate([own, before], axis=1)


def lag_table(shaping):
    lags = shaping.shape[1]
    line = jnp.concatenate([jnp.zeros((1, TILE), F32), shaping, jnp.zeros((1, TILE), F32)], axis=1)
    rolled = pltpu.roll(
        jnp.broadcast_to(line, (TILE, lags + 2 * TILE)), 0, 1, stride=1, stride_axis=0
    )
    blocks = []
    for block in range(lags // TILE + 1):
        at = lags + TILE - TILE * block
        blocks.append(rolled[:, at : at + TILE])
    return blocks


def in_hbm(x):
    return pltpu.with_memory_space_constraint(x, pltpu.HBM)


def zigzag(step, size):
    half = (step + 1) // 2
    away = jnp.where(step % 2 == 0, half, -half)
    return lax.rem(size // 2 + away + size, size)


def exchange_kernel(
    last_row, rows_y, rows_z, charge_ref, row_ref, column_ref, bin_ref, owner_ref, count_ref, shaping_ref,
    out_ref, table_ref, floats, ints, counts, line, rows, table, load_sem, send_sem, recv_sem,
):
    slabs = rows.shape[0]
    me = lax.axis_index("tm")
    group = lax.axis_index("pad")
    my_y, my_z = me // rows_z, lax.rem(me, rows_z)
    loads = [
        pltpu.make_async_copy(source, target, load_sem.at[index])
        for index, (source, target) in enumerate(
            (
                (charge_ref, floats),
                (row_ref, ints.at[0]),
                (column_ref, ints.at[1]),
                (bin_ref, ints.at[2]),
                (owner_ref, ints.at[3]),
                (count_ref, counts),
                (shaping_ref, line),
            )
        )
    ]
    for load in loads:
        load.start()

    def peer_of(step):
        z = lax.rem(my_z + zigzag(step // rows_y, rows_z), rows_z)
        y = lax.rem(my_y + zigzag(lax.rem(step, rows_y), rows_y), rows_y)
        return y * rows_z + z

    barrier = pltpu.get_barrier_semaphore()

    def greet(step, carry):
        pl.semaphore_signal(
            barrier, inc=1, device_id=(peer_of(step), group), device_id_type=pl.DeviceIdType.MESH
        )
        return carry

    lax.fori_loop(0, slabs - 1, greet, 0)
    for load in loads:
        load.wait()
    rows[...] = route_rows(
        last_row, slabs, floats[...], ints[0], ints[1], ints[2], ints[3], counts[...]
    )
    for index, block in enumerate(lag_table(line[...])):
        high, low = split(block)
        table[0, TILE * index : TILE * (index + 1)] = high
        table[1, TILE * index : TILE * (index + 1)] = low
    store = pltpu.make_async_copy(table, table_ref, load_sem.at[0])
    store.start()
    out_ref[pl.ds(me, 1)] = rows[pl.ds(me, 1)]
    pl.semaphore_wait(barrier, slabs - 1)

    def send(step, carry):
        peer = peer_of(step)
        pltpu.make_async_remote_copy(
            src_ref=rows.at[pl.ds(peer, 1)],
            dst_ref=out_ref.at[pl.ds(me, 1)],
            send_sem=send_sem,
            recv_sem=recv_sem,
            device_id=(peer, group),
            device_id_type=pl.DeviceIdType.MESH,
        ).start()
        return carry

    lax.fori_loop(0, slabs - 1, send, 0)
    some = rows.at[pl.ds(0, slabs - 1)]
    there = out_ref.at[pl.ds(0, slabs - 1)]
    pltpu.make_async_copy(some, there, recv_sem).wait()
    pltpu.make_async_copy(some, there, send_sem).wait()
    store.wait()


def exchange(charge, row, column, moment, owner, count, shaping, slabs, last_row, rows_y):
    clusters, lags = charge.shape[1], shaping.shape[1]
    return pl.pallas_call(
        functools.partial(exchange_kernel, last_row, rows_y, slabs // rows_y),
        out_shape=(
            jax.ShapeDtypeStruct((slabs, 2 * HALF), F32),
            jax.ShapeDtypeStruct((2, lags + TILE, TILE), BF16),
        ),
        in_specs=[pl.BlockSpec(memory_space=pltpu.HBM)] * 7,
        out_specs=(pl.BlockSpec(memory_space=pltpu.VMEM), pl.BlockSpec(memory_space=pl.ANY)),
        scratch_shapes=[
            pltpu.VMEM((1, clusters), F32),
            pltpu.VMEM((4, 1, clusters), jnp.int32),
            pltpu.VMEM(count.shape, jnp.int32),
            pltpu.VMEM((1, lags), F32),
            pltpu.VMEM((slabs, 2 * HALF), F32),
            pltpu.VMEM((2, lags + TILE, TILE), BF16),
            pltpu.SemaphoreType.DMA((7,)),
            pltpu.SemaphoreType.DMA,
            pltpu.SemaphoreType.DMA,
        ],
        compiler_params=pltpu.CompilerParams(
            collective_id=0, has_side_effects=True, vmem_limit_bytes=16 * 1024 * 1024
        ),
        name="exchange",
    )(*(in_hbm(x) for x in (charge, row, column, moment, owner, count, shaping)))


def slot_fields(received):
    flipped = jnp.transpose(received)
    half = CAP // 2
    found = []
    for slab in range(2):
        found.append([])
        for field in range(FIELDS):
            at = HALF * slab + CAP * field
            found[-1].append(
                jnp.concatenate([flipped[at : at + half], flipped[at + half : at + CAP]], axis=1)
            )
    return found


def hit_rows(moments, slot, bins):
    slabs = moments.shape[0]
    lane = lax.broadcasted_iota(jnp.int32, (slabs, LANES), 1).astype(F32)
    at = (slot % 2) * (CAP // 2) + slot // 2
    block = jnp.floor(moments * (1.0 / LANES))
    block, inner = (
        jnp.broadcast_to(d[:, at : at + 1], (slabs, LANES)) for d in (block, moments - LANES * block)
    )
    row = jnp.where(inner == lane, 1.0, 0.0).astype(BF16)
    block = block.astype(BF16)
    zero = jnp.zeros((slabs, LANES), BF16)
    return [jnp.where(block == float(k), row, zero) for k in range(bins // LANES)]


def keep(refs, at, grid, to):
    top = grid.astype(BF16)
    rows, width = grid.shape
    refs[0][at : at + rows, to : to + width] = top
    refs[1][at : at + rows, to : to + width] = grid.astype(F8)
    refs[2][at : at + rows, to : to + width] = ((grid - top.astype(F32)) * GRID_LOW).astype(F8)


def deposit_kernel(
    row_count, bins, recv_ref, high, high8, low8, sides_ref, wides, wides8, hits, hits8, send_sem, recv_sem
):
    slabs = recv_ref.shape[0]
    groups = lax.axis_size("pad")
    me = lax.axis_index("tm")
    group = lax.axis_index("pad")
    above = lax.rem(group + 1, groups)
    below = lax.rem(group + groups - 1, groups)
    barrier = pltpu.get_barrier_semaphore()
    for side in (above, below):
        pl.semaphore_signal(barrier, inc=1, device_id=(me, side), device_id_type=pl.DeviceIdType.MESH)
    pairs = CAP // 2
    cells = row_count * STRIDE
    pad = lax.broadcasted_iota(jnp.int32, (STRIDE, 2 * slabs), 0)
    fields = slot_fields(recv_ref[...])
    copies = []
    for slab in range(2):
        charge, row, column, _ = fields[slab]
        charge = charge * GRID
        top = charge.astype(BF16).astype(F32)
        rest = (charge - top) * CHARGE_LOW
        for pair in range(pairs):
            lanes = slice(2 * slabs * pair, 2 * slabs * (pair + 1))
            for lead in range(0, row_count, 4):
                count = min(4, row_count - lead)
                size = count * STRIDE
                pads = jnp.concatenate([pad] * count, axis=0).astype(F32).astype(BF16)
                there = pads == jnp.broadcast_to(column[pair : pair + 1], (size, 2 * slabs)).astype(BF16)
                blank = jnp.zeros((size, 2 * slabs), BF16)
                for part, target in ((top, wides), (rest, wides8)):
                    lines = []
                    for r in range(lead, lead + count):
                        value = jnp.where(row[pair : pair + 1] == float(r), part[pair : pair + 1], 0.0)
                        lines.append(jnp.broadcast_to(value, (STRIDE, 2 * slabs)))
                    values = jnp.concatenate(lines, axis=0).astype(BF16)
                    target[slab, lead * STRIDE : lead * STRIDE + size, lanes] = jnp.where(
                        there, values, blank
                    ).astype(target.dtype)
        at = HALF * slab + CAP * 3
        moments = recv_ref[:, at : at + CAP]
        for slot in range(CAP):
            for k, piece in enumerate(hit_rows(moments, slot, bins)):
                there = slice(slabs * slot, slabs * (slot + 1))
                hits[slab, there, LANES * k : LANES * (k + 1)] = piece
                hits8[slab, there, LANES * k : LANES * (k + 1)] = piece.astype(F8)
        if slab == 0:
            pl.semaphore_wait(barrier, 2)
            for index, (side, place) in enumerate(((above, 0), (below, 1))):
                copies.append(
                    pltpu.make_async_remote_copy(
                        src_ref=recv_ref,
                        dst_ref=sides_ref.at[place],
                        send_sem=send_sem.at[index],
                        recv_sem=recv_sem.at[index],
                        device_id=(me, side),
                        device_id_type=pl.DeviceIdType.MESH,
                    )
                )
                copies[-1].start()
        grid = jnp.dot(wides[slab], hits[slab], preferred_element_type=F32)
        grid += (1.0 / CHARGE_LOW) * jnp.dot(wides8[slab], hits8[slab], preferred_element_type=F32)
        keep((high, high8, low8), 0, grid, bins * (1 - slab))
    for copy in copies:
        copy.wait()

    @pl.when(group == 0)
    def _():
        sides_ref[0] = jnp.zeros(sides_ref.shape[1:], F32)

    @pl.when(group == groups - 1)
    def _():
        sides_ref[1] = jnp.zeros(sides_ref.shape[1:], F32)


def deposit(recv, row_count, bins):
    slabs, width = recv.shape
    cells = row_count * STRIDE
    grid = (cells, 2 * bins)
    slots = CAP * slabs
    return pl.pallas_call(
        functools.partial(deposit_kernel, row_count, bins),
        out_shape=(
            jax.ShapeDtypeStruct(grid, BF16),
            jax.ShapeDtypeStruct(grid, F8),
            jax.ShapeDtypeStruct(grid, F8),
            jax.ShapeDtypeStruct((2, slabs, width), F32),
        ),
        in_specs=[pl.BlockSpec(memory_space=pltpu.VMEM)],
        out_specs=(pl.BlockSpec(memory_space=pltpu.VMEM),) * 4,
        scratch_shapes=[
            pltpu.VMEM((2, cells, slots), BF16),
            pltpu.VMEM((2, cells, slots), F8),
            pltpu.VMEM((2, slots, bins), BF16),
            pltpu.VMEM((2, slots, bins), F8),
            pltpu.SemaphoreType.DMA((2,)),
            pltpu.SemaphoreType.DMA((2,)),
        ],
        compiler_params=pltpu.CompilerParams(
            collective_id=1, has_side_effects=True, vmem_limit_bytes=36 * 1024 * 1024
        ),
        name="deposit",
    )(recv)


def shape_kernel(
    row_count, bins, high, high8, low8, sides_ref, table_ref, weights_ref, out_ref,
    edge_high, edge_high8, edge_low8, table, table8, shaped, edges, held, staged, response_ref,
    table_sem, weights_sem, out_sem,
):
    fetch = pltpu.make_async_copy(weights_ref, response_ref, weights_sem)
    fetch.start()
    load = pltpu.make_async_copy(table_ref, table, table_sem)
    load.start()
    slabs = sides_ref.shape[1]
    pairs = CAP // 2
    cells = row_count * STRIDE
    pad = lax.broadcasted_iota(jnp.int32, (STRIDE, 2 * slabs), 0)
    place = 2 * lax.broadcasted_iota(jnp.int32, (pairs, 2 * slabs), 0) + (
        lax.broadcasted_iota(jnp.int32, (pairs, 2 * slabs), 1) // slabs
    )
    held[...] = jnp.zeros(held.shape, F32)
    needed = jnp.zeros((), F32)
    for index in range(2):
        fields = slot_fields(sides_ref[index])
        edge = 0.0 if index else float(row_count - 1)
        depth = (CAP - 1 - place if index else place) + 1
        for slab in range(2):
            charge, row, column, _ = fields[slab]
            kept = jnp.where(row == edge, charge * GRID, 0.0)
            needed = jnp.maximum(needed, jnp.max(jnp.where(kept != 0.0, depth, 0).astype(F32)))
            edges[index, slab, 0] = kept
            edges[index, slab, 1] = column
    chunks = (needed.astype(jnp.int32) + 3) // 4
    for number in range(CAP // 4):

        @pl.when(number < chunks)
        def _():
            for index in range(2):
                first = CAP - 4 - 4 * number if index else 4 * number
                for slab in range(2):
                    weights = []
                    for pair in (first // 2, first // 2 + 1):
                        there = pad == edges[index, slab, 1, pair : pair + 1].astype(jnp.int32)
                        weights.append(jnp.where(there, edges[index, slab, 0, pair : pair + 1], 0.0))
                    top = jnp.concatenate(weights, axis=1)
                    rest = top - top.astype(BF16).astype(F32)
                    left = jnp.concatenate([top, rest], axis=0).astype(BF16)
                    at = HALF * slab + CAP * 3
                    moments = sides_ref[index, :, at : at + CAP]
                    right = jnp.concatenate(
                        [jnp.concatenate(hit_rows(moments, first + k, bins), axis=1) for k in range(4)], axis=0
                    )
                    both = jnp.dot(left, right, preferred_element_type=F32)
                    at = bins * (1 - slab)
                    held[index, :, at : at + bins] += both[:STRIDE] + both[STRIDE:]

    keep((edge_high, edge_high8, edge_low8), 0, held[...].reshape(2 * STRIDE, 2 * bins), 0)

    load.wait()
    table8[0] = (table[0].astype(F32) * TABLE_HIGH).astype(F8)
    table8[1] = (table[1].astype(F32) * TABLE_LOW).astype(F8)
    depth = table.shape[1]
    steps = bins // TILE
    fetch.wait()
    weights = [[response_ref[a, b] * (1.0 / GRID) for b in range(3)] for a in range(3)]
    copies = []
    for step in range(steps + 1):
        if step < steps:
            near = slice(TILE * step, TILE * step + depth)
            for at, rows, refs in (
                (0, cells, (high, high8, low8)),
                (cells, 2 * STRIDE, (edge_high, edge_high8, edge_low8)),
            ):
                fine = jnp.dot(
                    jnp.concatenate([refs[2][:, near], refs[1][:, near]], axis=1),
                    table8[...].reshape(2 * depth, TILE),
                    preferred_element_type=F32,
                )
                shaped[step % 2, at : at + rows] = (
                    jnp.dot(refs[0][:, near], table[0], preferred_element_type=F32) + FINE * fine
                )
        if step > 0:
            done = step - 1
            if done >= 2:
                copies[done - 2].wait()
            for r in range(row_count):
                near = []
                for a in range(3):
                    at = (r + a - 1) * STRIDE if 0 < r + a <= row_count else cells + STRIDE * (r + a > 0)
                    near.append(shaped[done % 2, at : at + STRIDE])
                sums = []
                for b in range(3):
                    sums.append(weights[0][b] * near[0] + weights[1][b] * near[1] + weights[2][b] * near[2])
                total = sums[1] + pltpu.roll(sums[0], 1, 0) + pltpu.roll(sums[2], STRIDE - 1, 0)
                staged[done % 2, r] = total[:PPR]
            copies.append(
                pltpu.make_async_copy(
                    staged.at[done % 2],
                    out_ref.at[:, :, pl.ds(TILE * done, TILE)],
                    out_sem.at[done % 2],
                )
            )
            copies[-1].start()
    for copy in copies[-2:]:
        copy.wait()


def shape_and_spread(high, high8, low8, sides, table, response, row_count, bins):
    slabs = sides.shape[1]
    edge = (2 * STRIDE, 2 * bins)
    vmem = pl.BlockSpec(memory_space=pltpu.VMEM)
    return pl.pallas_call(
        functools.partial(shape_kernel, row_count, bins),
        out_shape=jax.ShapeDtypeStruct((row_count, PPR, bins), F32),
        in_specs=[vmem, vmem, vmem, vmem, pl.BlockSpec(memory_space=pl.ANY), pl.BlockSpec(memory_space=pltpu.HBM)],
        out_specs=pl.BlockSpec(memory_space=pl.ANY),
        scratch_shapes=[
            pltpu.VMEM(edge, BF16),
            pltpu.VMEM(edge, F8),
            pltpu.VMEM(edge, F8),
            pltpu.VMEM(table.shape, BF16),
            pltpu.VMEM(table.shape, F8),
            pltpu.VMEM((2, row_count * STRIDE + 2 * STRIDE, TILE), F32),
            pltpu.VMEM((2, 2, 2, CAP // 2, 2 * slabs), F32),
            pltpu.VMEM((2, STRIDE, 2 * bins), F32),
            pltpu.VMEM((2, row_count, PPR, TILE), F32),
            pltpu.SMEM(response.shape, F32),
            pltpu.SemaphoreType.DMA,
            pltpu.SemaphoreType.DMA,
            pltpu.SemaphoreType.DMA((2,)),
        ],
        compiler_params=pltpu.CompilerParams(vmem_limit_bytes=36 * 1024 * 1024),
        name="shape",
    )(high, high8, low8, sides, table, in_hbm(response))


def solution(mesh):
    slabs, groups = mesh.shape["tm"], mesh.shape["pad"]
    row_count = PROWS // groups
    bins = 1024
    rows_y = 4 if slabs % 4 == 0 else 1

    def body(charge, pad_row, pad_column, time_bin, slab_owner, block_count, shaping, response):
        owner = slab_owner.reshape(1, slab_owner.shape[1])
        line = shaping.reshape(1, shaping.shape[0])
        received, table = exchange(
            charge, pad_row, pad_column, time_bin, owner, block_count, line, slabs, row_count - 1, rows_y
        )
        high, high8, low8, sides = deposit(received, row_count, bins)
        return shape_and_spread(high, high8, low8, sides, table, response, row_count, bins)

    in_specs = (P("pad", "tm"),) * 4 + (P("pad", "tm", None), P("pad", "tm"), P(), P())
    return jax.shard_map(
        body, mesh=mesh, in_specs=in_specs, out_specs=P("pad", None, "tm"), check_vma=False
    )
```

```python
import functools

import jax
import jax.numpy as jnp
from jax import lax
from jax.experimental import pallas as pl
from jax.experimental.pallas import tpu as pltpu
from jax.sharding import PartitionSpec as P

PROWS = 80
PPR = 66
STRIDE = 72
CAP = 16
FIELDS = 4
HALF = FIELDS * CAP
F32 = jnp.float32
BF16 = jnp.bfloat16
F8 = jnp.float8_e4m3fn
GRID, GRID_LOW = 2.0**-3, 2.0**8
TABLE_HIGH, TABLE_LOW = 2.0**7, 2.0**15
CHARGE_LOW = 2.0**17
FINE = 2.0**-15
LANES = 128
TILE = 256
NT = (((1,), (1,)), ((), ()))


def split(x):
    high = x.astype(BF16)
    return high, (x - high.astype(F32)).astype(BF16)


def route_rows(last_row, slabs, charge, row, column, moment, owner, count):
    clusters = charge.shape[1]
    lane = lax.broadcasted_iota(jnp.int32, (1, clusters), 1)
    limit = jnp.zeros((1, clusters), jnp.int32)
    for block in range(clusters // LANES):
        limit = jnp.where(lane // LANES == block, count[:, block : block + 1], limit)
    live = lane % LANES < limit
    owner = jnp.where(live, owner, slabs)
    mine = owner == lax.broadcasted_iota(jnp.int32, (slabs, clusters), 0)
    middle = (last_row + 1) // 2
    order = (
        row == last_row,
        jnp.logical_and(row >= middle, row < last_row),
        jnp.logical_and(row < middle, row > 0),
        row == 0,
    )
    kinds = [jnp.where(jnp.logical_and(mine, kind), 1.0, 0.0) for kind in order]
    stacked = jnp.concatenate(kinds, axis=0).astype(BF16)
    earlier = (
        lax.broadcasted_iota(jnp.int32, (clusters, clusters), 0)
        < lax.broadcasted_iota(jnp.int32, (clusters, clusters), 1)
    ).astype(F32).astype(BF16)
    ranks = jnp.dot(stacked, earlier, preferred_element_type=F32)
    ranks = [ranks[slabs * k : slabs * (k + 1)] for k in range(4)]
    firsts = jnp.sum(kinds[0], axis=1, keepdims=True)
    lasts = jnp.sum(kinds[3], axis=1, keepdims=True)
    places = (
        kinds[0] * ranks[0]
        + kinds[1] * (firsts + ranks[1])
        + kinds[2] * ((CAP - 1) - lasts - ranks[2])
        + kinds[3] * ((CAP - 1) - ranks[3])
    )
    place = jnp.sum(places, axis=0, keepdims=True)
    slot = lax.broadcasted_iota(jnp.int32, (CAP, clusters), 0)
    half = CAP // 2
    here = place == (2 * (slot % half) + slot // half).astype(F32)
    fields = (charge, row.astype(F32), column.astype(F32), moment.astype(F32))
    spread_out = jnp.concatenate([jnp.where(here, field, 0.0) for field in fields], axis=0)
    own = lax.dot_general(
        jnp.where(mine, 1.0, 0.0), spread_out, NT, precision=lax.Precision.HIGHEST, preferred_element_type=F32
    )
    slab = lax.broadcasted_iota(jnp.int32, own.shape, 0)
    before = jnp.where(slab == 0, 0.0, pltpu.roll(own, 1, 0))
    return jnp.concatenate([own, before], axis=1)


def lag_table(shaping):
    lags = shaping.shape[1]
    line = jnp.concatenate([jnp.zeros((1, TILE), F32), shaping, jnp.zeros((1, TILE), F32)], axis=1)
    rolled = pltpu.roll(
        jnp.broadcast_to(line, (TILE, lags + 2 * TILE)), 0, 1, stride=1, stride_axis=0
    )
    blocks = []
    for block in range(lags // TILE + 1):
        at = lags + TILE - TILE * block
        blocks.append(rolled[:, at : at + TILE])
    return blocks


def in_hbm(x):
    return pltpu.with_memory_space_constraint(x, pltpu.HBM)


def zigzag(step, size):
    half = (step + 1) // 2
    away = jnp.where(step % 2 == 0, half, -half)
    return lax.rem(size // 2 + away + size, size)


def exchange_kernel(
    last_row, rows_y, rows_z, charge_ref, row_ref, column_ref, bin_ref, owner_ref, count_ref, shaping_ref,
    out_ref, table_ref, floats, ints, counts, line, rows, table, load_sem, send_sem, recv_sem,
):
    slabs = rows.shape[0]
    me = lax.axis_index("tm")
    group = lax.axis_index("pad")
    my_y, my_z = me // rows_z, lax.rem(me, rows_z)
    loads = [
        pltpu.make_async_copy(source, target, load_sem.at[index])
        for index, (source, target) in enumerate(
            (
                (charge_ref, floats),
                (row_ref, ints.at[0]),
                (column_ref, ints.at[1]),
                (bin_ref, ints.at[2]),
                (owner_ref, ints.at[3]),
                (count_ref, counts),
                (shaping_ref, line),
            )
        )
    ]
    for load in loads:
        load.start()

    def peer_of(step):
        z = lax.rem(my_z + zigzag(step // rows_y, rows_z), rows_z)
        y = lax.rem(my_y + zigzag(lax.rem(step, rows_y), rows_y), rows_y)
        return y * rows_z + z

    barrier = pltpu.get_barrier_semaphore()

    def greet(step, carry):
        pl.semaphore_signal(
            barrier, inc=1, device_id=(peer_of(step), group), device_id_type=pl.DeviceIdType.MESH
        )
        return carry

    lax.fori_loop(0, slabs - 1, greet, 0)
    for load in loads:
        load.wait()
    rows[...] = route_rows(
        last_row, slabs, floats[...], ints[0], ints[1], ints[2], ints[3], counts[...]
    )
    for index, block in enumerate(lag_table(line[...])):
        high, low = split(block)
        table[0, TILE * index : TILE * (index + 1)] = high
        table[1, TILE * index : TILE * (index + 1)] = low
    store = pltpu.make_async_copy(table, table_ref, load_sem.at[0])
    store.start()
    out_ref[pl.ds(me, 1)] = rows[pl.ds(me, 1)]
    pl.semaphore_wait(barrier, slabs - 1)

    def send(step, carry):
        peer = peer_of(step)
        pltpu.make_async_remote_copy(
            src_ref=rows.at[pl.ds(peer, 1)],
            dst_ref=out_ref.at[pl.ds(me, 1)],
            send_sem=send_sem,
            recv_sem=recv_sem,
            device_id=(peer, group),
            device_id_type=pl.DeviceIdType.MESH,
        ).start()
        return carry

    lax.fori_loop(0, slabs - 1, send, 0)
    some = rows.at[pl.ds(0, slabs - 1)]
    there = out_ref.at[pl.ds(0, slabs - 1)]
    pltpu.make_async_copy(some, there, recv_sem).wait()
    pltpu.make_async_copy(some, there, send_sem).wait()
    store.wait()


def exchange(charge, row, column, moment, owner, count, shaping, slabs, last_row, rows_y):
    clusters, lags = charge.shape[1], shaping.shape[1]
    return pl.pallas_call(
        functools.partial(exchange_kernel, last_row, rows_y, slabs // rows_y),
        out_shape=(
            jax.ShapeDtypeStruct((slabs, 2 * HALF), F32),
            jax.ShapeDtypeStruct((2, lags + TILE, TILE), BF16),
        ),
        in_specs=[pl.BlockSpec(memory_space=pltpu.HBM)] * 7,
        out_specs=(pl.BlockSpec(memory_space=pltpu.VMEM), pl.BlockSpec(memory_space=pl.ANY)),
        scratch_shapes=[
            pltpu.VMEM((1, clusters), F32),
            pltpu.VMEM((4, 1, clusters), jnp.int32),
            pltpu.VMEM(count.shape, jnp.int32),
            pltpu.VMEM((1, lags), F32),
            pltpu.VMEM((slabs, 2 * HALF), F32),
            pltpu.VMEM((2, lags + TILE, TILE), BF16),
            pltpu.SemaphoreType.DMA((7,)),
            pltpu.SemaphoreType.DMA,
            pltpu.SemaphoreType.DMA,
        ],
        compiler_params=pltpu.CompilerParams(
            collective_id=0, has_side_effects=True, vmem_limit_bytes=16 * 1024 * 1024
        ),
        name="exchange",
    )(*(in_hbm(x) for x in (charge, row, column, moment, owner, count, shaping)))


def slot_fields(received):
    flipped = jnp.transpose(received)
    half = CAP // 2
    found = []
    for slab in range(2):
        found.append([])
        for field in range(FIELDS):
            at = HALF * slab + CAP * field
            found[-1].append(
                jnp.concatenate([flipped[at : at + half], flipped[at + half : at + CAP]], axis=1)
            )
    return found


def hit_rows(moments, slot, bins):
    slabs = moments.shape[0]
    lane = lax.broadcasted_iota(jnp.int32, (slabs, LANES), 1).astype(F32)
    at = (slot % 2) * (CAP // 2) + slot // 2
    block = jnp.floor(moments * (1.0 / LANES))
    block, inner = (
        jnp.broadcast_to(d[:, at : at + 1], (slabs, LANES)) for d in (block, moments - LANES * block)
    )
    row = jnp.where(inner == lane, 1.0, 0.0).astype(BF16)
    block = block.astype(BF16)
    zero = jnp.zeros((slabs, LANES), BF16)
    return [jnp.where(block == float(k), row, zero) for k in range(bins // LANES)]


def keep(refs, at, grid, to):
    top = grid.astype(BF16)
    rows, width = grid.shape
    refs[0][at : at + rows, to : to + width] = top
    refs[1][at : at + rows, to : to + width] = grid.astype(F8)
    refs[2][at : at + rows, to : to + width] = ((grid - top.astype(F32)) * GRID_LOW).astype(F8)


def deposit_kernel(
    row_count, bins, recv_ref, high, high8, low8, sides_ref, wides, wides8, hits, hits8, send_sem, recv_sem
):
    slabs = recv_ref.shape[0]
    groups = lax.axis_size("pad")
    me = lax.axis_index("tm")
    group = lax.axis_index("pad")
    above = lax.rem(group + 1, groups)
    below = lax.rem(group + groups - 1, groups)
    barrier = pltpu.get_barrier_semaphore()
    for side in (above, below):
        pl.semaphore_signal(barrier, inc=1, device_id=(me, side), device_id_type=pl.DeviceIdType.MESH)
    pairs = CAP // 2
    cells = row_count * STRIDE
    pad = lax.broadcasted_iota(jnp.int32, (STRIDE, 2 * slabs), 0)
    fields = slot_fields(recv_ref[...])
    copies, grids = [], []
    for slab in range(2):
        charge, row, column, _ = fields[slab]
        charge = charge * GRID
        top = charge.astype(BF16).astype(F32)
        rest = (charge - top) * CHARGE_LOW
        for pair in range(pairs):
            lanes = slice(2 * slabs * pair, 2 * slabs * (pair + 1))
            for lead in range(0, row_count, 4):
                count = min(4, row_count - lead)
                size = count * STRIDE
                pads = jnp.concatenate([pad] * count, axis=0).astype(F32).astype(BF16)
                there = pads == jnp.broadcast_to(column[pair : pair + 1], (size, 2 * slabs)).astype(BF16)
                blank = jnp.zeros((size, 2 * slabs), BF16)
                for part, target in ((top, wides), (rest, wides8)):
                    lines = []
                    for r in range(lead, lead + count):
                        value = jnp.where(row[pair : pair + 1] == float(r), part[pair : pair + 1], 0.0)
                        lines.append(jnp.broadcast_to(value, (STRIDE, 2 * slabs)))
                    values = jnp.concatenate(lines, axis=0).astype(BF16)
                    target[slab, lead * STRIDE : lead * STRIDE + size, lanes] = jnp.where(
                        there, values, blank
                    ).astype(target.dtype)
        at = HALF * slab + CAP * 3
        moments = recv_ref[:, at : at + CAP]
        for slot in range(CAP):
            for k, piece in enumerate(hit_rows(moments, slot, bins)):
                there = slice(slabs * slot, slabs * (slot + 1))
                hits[slab, there, LANES * k : LANES * (k + 1)] = piece
                hits8[slab, there, LANES * k : LANES * (k + 1)] = piece.astype(F8)
        if slab == 1:
            keep((high, high8, low8), 0, grids[0], bins)
            pl.semaphore_wait(barrier, 2)
            for index, (side, place) in enumerate(((above, 0), (below, 1))):
                copies.append(
                    pltpu.make_async_remote_copy(
                        src_ref=recv_ref,
                        dst_ref=sides_ref.at[place],
                        send_sem=send_sem.at[index],
                        recv_sem=recv_sem.at[index],
                        device_id=(me, side),
                        device_id_type=pl.DeviceIdType.MESH,
                    )
                )
                copies[-1].start()
        grid = jnp.dot(wides[slab], hits[slab], preferred_element_type=F32)
        grid += (1.0 / CHARGE_LOW) * jnp.dot(wides8[slab], hits8[slab], preferred_element_type=F32)
        grids.append(grid)
    keep((high, high8, low8), 0, grids[1], 0)
    for copy in copies:
        copy.wait()

    @pl.when(group == 0)
    def _():
        sides_ref[0] = jnp.zeros(sides_ref.shape[1:], F32)

    @pl.when(group == groups - 1)
    def _():
        sides_ref[1] = jnp.zeros(sides_ref.shape[1:], F32)


def deposit(recv, row_count, bins):
    slabs, width = recv.shape
    cells = row_count * STRIDE
    grid = (cells, 2 * bins)
    slots = CAP * slabs
    return pl.pallas_call(
        functools.partial(deposit_kernel, row_count, bins),
        out_shape=(
            jax.ShapeDtypeStruct(grid, BF16),
            jax.ShapeDtypeStruct(grid, F8),
            jax.ShapeDtypeStruct(grid, F8),
            jax.ShapeDtypeStruct((2, slabs, width), F32),
        ),
        in_specs=[pl.BlockSpec(memory_space=pltpu.VMEM)],
        out_specs=(pl.BlockSpec(memory_space=pltpu.VMEM),) * 4,
        scratch_shapes=[
            pltpu.VMEM((2, cells, slots), BF16),
            pltpu.VMEM((2, cells, slots), F8),
            pltpu.VMEM((2, slots, bins), BF16),
            pltpu.VMEM((2, slots, bins), F8),
            pltpu.SemaphoreType.DMA((2,)),
            pltpu.SemaphoreType.DMA((2,)),
        ],
        compiler_params=pltpu.CompilerParams(
            collective_id=1, has_side_effects=True, vmem_limit_bytes=36 * 1024 * 1024
        ),
        name="deposit",
    )(recv)


def shape_kernel(
    row_count, bins, high, high8, low8, sides_ref, table_ref, weights_ref, out_ref,
    edge_high, edge_high8, edge_low8, table, table8, shaped, edges, held, staged, response_ref,
    table_sem, weights_sem, out_sem,
):
    fetch = pltpu.make_async_copy(weights_ref, response_ref, weights_sem)
    fetch.start()
    load = pltpu.make_async_copy(table_ref, table, table_sem)
    load.start()
    slabs = sides_ref.shape[1]
    pairs = CAP // 2
    cells = row_count * STRIDE
    pad = lax.broadcasted_iota(jnp.int32, (STRIDE, 2 * slabs), 0)
    place = 2 * lax.broadcasted_iota(jnp.int32, (pairs, 2 * slabs), 0) + (
        lax.broadcasted_iota(jnp.int32, (pairs, 2 * slabs), 1) // slabs
    )
    held[...] = jnp.zeros(held.shape, F32)
    needed = jnp.zeros((), F32)
    for index in range(2):
        fields = slot_fields(sides_ref[index])
        edge = 0.0 if index else float(row_count - 1)
        depth = (CAP - 1 - place if index else place) + 1
        for slab in range(2):
            charge, row, column, _ = fields[slab]
            kept = jnp.where(row == edge, charge * GRID, 0.0)
            needed = jnp.maximum(needed, jnp.max(jnp.where(kept != 0.0, depth, 0).astype(F32)))
            edges[index, slab, 0] = kept
            edges[index, slab, 1] = column
    chunks = (needed.astype(jnp.int32) + 3) // 4
    for number in range(CAP // 4):

        @pl.when(number < chunks)
        def _():
            for index in range(2):
                first = CAP - 4 - 4 * number if index else 4 * number
                for slab in range(2):
                    weights = []
                    for pair in (first // 2, first // 2 + 1):
                        there = pad == edges[index, slab, 1, pair : pair + 1].astype(jnp.int32)
                        weights.append(jnp.where(there, edges[index, slab, 0, pair : pair + 1], 0.0))
                    top = jnp.concatenate(weights, axis=1)
                    rest = top - top.astype(BF16).astype(F32)
                    left = jnp.concatenate([top, rest], axis=0).astype(BF16)
                    at = HALF * slab + CAP * 3
                    moments = sides_ref[index, :, at : at + CAP]
                    right = jnp.concatenate(
                        [jnp.concatenate(hit_rows(moments, first + k, bins), axis=1) for k in range(4)], axis=0
                    )
                    both = jnp.dot(left, right, preferred_element_type=F32)
                    at = bins * (1 - slab)
                    held[index, :, at : at + bins] += both[:STRIDE] + both[STRIDE:]

    keep((edge_high, edge_high8, edge_low8), 0, held[...].reshape(2 * STRIDE, 2 * bins), 0)

    load.wait()
    table8[0] = (table[0].astype(F32) * TABLE_HIGH).astype(F8)
    table8[1] = (table[1].astype(F32) * TABLE_LOW).astype(F8)
    depth = table.shape[1]
    steps = bins // TILE
    fetch.wait()
    weights = [[response_ref[a, b] * (1.0 / GRID) for b in range(3)] for a in range(3)]
    copies = []
    for step in range(steps + 1):
        if step < steps:
            near = slice(TILE * step, TILE * step + depth)
            for at, rows, refs in (
                (0, cells, (high, high8, low8)),
                (cells, 2 * STRIDE, (edge_high, edge_high8, edge_low8)),
            ):
                fine = jnp.dot(
                    jnp.concatenate([refs[2][:, near], refs[1][:, near]], axis=1),
                    table8[...].reshape(2 * depth, TILE),
                    preferred_element_type=F32,
                )
                shaped[step % 2, at : at + rows] = (
                    jnp.dot(refs[0][:, near], table[0], preferred_element_type=F32) + FINE * fine
                )
        if step > 0:
            done = step - 1
            if done >= 2:
                copies[done - 2].wait()
            parts = ((0, row_count),) if step < steps else ((0, row_count // 2), (row_count // 2, row_count))
            for part, (begin, end) in enumerate(parts):
                for r in range(begin, end):
                    near = []
                    for a in range(3):
                        at = (r + a - 1) * STRIDE if 0 < r + a <= row_count else cells + STRIDE * (r + a > 0)
                        near.append(shaped[done % 2, at : at + STRIDE])
                    sums = []
                    for b in range(3):
                        sums.append(weights[0][b] * near[0] + weights[1][b] * near[1] + weights[2][b] * near[2])
                    total = sums[1] + pltpu.roll(sums[0], 1, 0) + pltpu.roll(sums[2], STRIDE - 1, 0)
                    staged[done % 2, r] = total[:PPR]
                copies.append(
                    pltpu.make_async_copy(
                        staged.at[done % 2, pl.ds(begin, end - begin)],
                        out_ref.at[pl.ds(begin, end - begin), :, pl.ds(TILE * done, TILE)],
                        out_sem.at[2 if part else done % 2],
                    )
                )
                copies[-1].start()
    for copy in copies[-3:]:
        copy.wait()


def shape_and_spread(high, high8, low8, sides, table, response, row_count, bins):
    slabs = sides.shape[1]
    edge = (2 * STRIDE, 2 * bins)
    vmem = pl.BlockSpec(memory_space=pltpu.VMEM)
    return pl.pallas_call(
        functools.partial(shape_kernel, row_count, bins),
        out_shape=jax.ShapeDtypeStruct((row_count, PPR, bins), F32),
        in_specs=[vmem, vmem, vmem, vmem, pl.BlockSpec(memory_space=pl.ANY), pl.BlockSpec(memory_space=pltpu.HBM)],
        out_specs=pl.BlockSpec(memory_space=pl.ANY),
        scratch_shapes=[
            pltpu.VMEM(edge, BF16),
            pltpu.VMEM(edge, F8),
            pltpu.VMEM(edge, F8),
            pltpu.VMEM(table.shape, BF16),
            pltpu.VMEM(table.shape, F8),
            pltpu.VMEM((2, row_count * STRIDE + 2 * STRIDE, TILE), F32),
            pltpu.VMEM((2, 2, 2, CAP // 2, 2 * slabs), F32),
            pltpu.VMEM((2, STRIDE, 2 * bins), F32),
            pltpu.VMEM((2, row_count, PPR, TILE), F32),
            pltpu.SMEM(response.shape, F32),
            pltpu.SemaphoreType.DMA,
            pltpu.SemaphoreType.DMA,
            pltpu.SemaphoreType.DMA((3,)),
        ],
        compiler_params=pltpu.CompilerParams(vmem_limit_bytes=36 * 1024 * 1024),
        name="shape",
    )(high, high8, low8, sides, table, in_hbm(response))


def solution(mesh):
    slabs, groups = mesh.shape["tm"], mesh.shape["pad"]
    row_count = PROWS // groups
    bins = 1024
    rows_y = 4 if slabs % 4 == 0 else 1

    def body(charge, pad_row, pad_column, time_bin, slab_owner, block_count, shaping, response):
        owner = slab_owner.reshape(1, slab_owner.shape[1])
        line = shaping.reshape(1, shaping.shape[0])
        received, table = exchange(
            charge, pad_row, pad_column, time_bin, owner, block_count, line, slabs, row_count - 1, rows_y
        )
        high, high8, low8, sides = deposit(received, row_count, bins)
        return shape_and_spread(high, high8, low8, sides, table, response, row_count, bins)

    in_specs = (P("pad", "tm"),) * 4 + (P("pad", "tm", None), P("pad", "tm"), P(), P())
    return jax.shard_map(
        body, mesh=mesh, in_specs=in_specs, out_specs=P("pad", None, "tm"), check_vma=False
    )
```
